1024 devices in a mesh: row: 8 (over y_lo, x), col: 128 (over z, y_hi, core).
Axes of the slice: x: 4, y: 4 (y_hi: 2, y_lo: 2; y = y_hi * 2 + y_lo), z: 32, core: 2. Of those that a mesh axis runs over, the one named last changes fastest.
Arguments:
- view_a: bfloat16 [1024, 8192], P('col', 'row'), may hold values from -30 to 30
- view_b: bfloat16 [1024, 8192], P('row', 'col'), may hold values from -30 to 30
Outputs:
- loss: float32 [], replicated
- grad_a: bfloat16 [1024, 8192], P('col', 'row')
- grad_b: bfloat16 [1024, 8192], P('row', 'col')
The draws below stay inside these ranges and needn't reach their ends.
All inputs are finite; a program needn't handle non-finite values.
Results may differ from the reference program's by a relative error of at most 0.0062.
Values may be sent and summed in bfloat16 or wider, within the bound.
A program may use at most 64 MiB of HBM per device.

```python
import jax
import jax.numpy as jnp
from jax import lax

F = 8192
IMAGES = 1024
N_ROW = 8


def shared_part(key):
    base = jax.random.fold_in(key, 11)
    return jax.random.normal(base, (IMAGES, F), jnp.float32)


def noise_ramp(key):
    position = lax.iota(jnp.int32, F).astype(jnp.float32) / (F - 1)
    lowest, highest = (0.3, 2.0)
    ramp = jnp.exp(jnp.log(lowest) + (jnp.log(highest) - jnp.log(lowest)) * position)
    jitter = jnp.exp(jax.random.uniform(jax.random.fold_in(key, 13), (F,), jnp.float32, -0.22, 0.22))
    return (ramp * jitter)[None, :]


def one_view(key, salt):
    common = shared_part(key)
    ramp = noise_ramp(key)
    noise = jax.random.normal(jax.random.fold_in(key, salt), (IMAGES, F), jnp.float32)
    scale = jnp.exp(jax.random.uniform(jax.random.fold_in(key, salt + 1), (1, F), jnp.float32, -1.2, 1.2))
    offset = 1.5 * jax.random.normal(jax.random.fold_in(key, salt + 2), (1, F), jnp.float32)
    values = offset + scale * (common + ramp * noise)
    return jnp.clip(values, -30.0, 30.0).astype(jnp.bfloat16)


def draw_view_a(key, part):
    return one_view(key, 21)


def draw_view_b(key, part):
    return one_view(key, 31)


def setup_inputs(seed: int = 0) -> dict:
    key_list = jax.random.split(jax.random.key(seed), 3)
    return {
        "view_a": draw_view_a(jax.random.fold_in(key_list[2], 71), 0),
        "view_b": draw_view_b(jax.random.fold_in(key_list[2], 71), 0),
    }


off_weight = 0.0051
epsilon = 1e-05

def normalize(values):
    values = values.astype(jnp.float32)
    center = lax.optimization_barrier(jnp.mean(values, 0))
    spread = lax.optimization_barrier(jnp.mean(jnp.square(values - center), 0))
    scaled = lax.rsqrt(spread + epsilon)
    return (((values - center) * scaled).astype(jnp.bfloat16), scaled)

def project(term, normed, scaled):
    normal_f = normed.astype(jnp.float32)
    return scaled * (term - lax.optimization_barrier(jnp.mean(term, 0)) - normal_f * lax.optimization_barrier(jnp.mean(term * normal_f, 0)))

def reference(view_a, view_b):
    normed_a, scaled_a = normalize(view_a)
    normed_b, scaled_b = normalize(view_b)
    width = F // N_ROW
    blocks_a = normed_a.reshape(IMAGES, N_ROW, width).transpose(1, 0, 2)
    columns = lax.iota(jnp.int32, F)

    def one_block(carry, inputs):
        loss_sum, term_b = carry
        index, block = inputs
        corr = lax.dot_general(block, normed_b, (((0,), (0,)), ((), ())), preferred_element_type=jnp.float32) / IMAGES
        rows = index * width + lax.iota(jnp.int32, width)
        diag = rows[:, None] == columns[None, :]
        part = jnp.sum(jnp.where(diag, jnp.square(1.0 - corr), off_weight * jnp.square(corr)))
        weights = jnp.where(diag, 2.0 * (corr - 1.0), 2.0 * off_weight * corr).astype(jnp.bfloat16)
        term_a = lax.dot_general(normed_b, weights, (((1,), (1,)), ((), ())), preferred_element_type=jnp.float32)
        term_b = term_b + jnp.dot(block, weights, preferred_element_type=jnp.float32)
        return ((loss_sum + part, term_b), term_a)
    start = (jnp.zeros((), jnp.float32), jnp.zeros((IMAGES, F), jnp.float32))
    indices = lax.iota(jnp.int32, N_ROW)
    (loss_sum, term_b), terms_a = lax.scan(one_block, start, (indices, blocks_a))
    term_a = terms_a.transpose(1, 0, 2).reshape(IMAGES, F)
    grad_a = project(term_a, normed_a, scaled_a).astype(jnp.bfloat16)
    grad_b = project(term_b, normed_b, scaled_b).astype(jnp.bfloat16)
    return (loss_sum / F, grad_a, grad_b)
```

```python
import functools

import jax
import jax.numpy as jnp
from jax import lax
from jax.experimental import pallas as pl
from jax.experimental.pallas import tpu as pltpu
from jax.sharding import Mesh
from jax.sharding import PartitionSpec as P

AXES = ("yl", "x", "z", "yh", "k")
ROW = ("yl", "x")
COL = ("z", "yh", "k")
MESH = pl.DeviceIdType.MESH

off_weight = 0.0051
epsilon = 1e-05
K = 2
LANES = 128
SUB = 8

f32 = jnp.float32
bf16 = jnp.bfloat16


def kernel(
    X, ZL, YH, ZH,
    a_ref, b_ref, loss_ref, ga_ref, gb_ref,
    ta, xa, pb, xf, na, nb,
    gp_a, gp_b, ra_a, ra_b, hs_a, hs_b, rb_a, rb_b, ms_a, ms_b, rg_a, rg_b,
    ds0, db0, ds1, db1, ss_a, sb_a, ss_b, sb_b, fs, fa, tb, tp,
    send, recv,
):
    R, M = ZH, ZL * YH
    N = R * K
    rows = M * SUB
    images = N * rows
    features = ZH * M * LANES
    yl, x, z, yh, k = (lax.axis_index(name) for name in AXES)
    r = yl * X + x
    zh, zl = z // ZL, z % ZL
    rho, m = r * K + k, zl * YH + yh
    s = m * K + k

    def device(r_, z_, yh_, k_):
        return (r_ // X, r_ % X, z_, yh_, k_)

    def near_row(p):
        return device(p // K, z, yh, p % K)

    def near_chip(p):
        return device(r, zh * ZL + p // YH, p % YH, k)

    def far_block(p):
        return device(r, p * ZL + zl, yh, k)

    def target(q):
        return device(zh, r * ZL + q // YH, q % YH, s // M)

    def source(b):
        s_ = k * M + b
        return device(zh, r * ZL + (s_ // K) // YH, (s_ // K) % YH, s_ % K)

    own = jnp.logical_and(zh == r, s // M == k)
    own_target, own_source = m, s % M

    barrier = pltpu.get_barrier_semaphore()

    def greet(n, me, peer):
        def one(t, c):
            pl.semaphore_signal(barrier, inc=1, device_id=peer(lax.rem(me + t, n)), device_id_type=MESH)
            return c

        lax.fori_loop(1, n, one, 0)

    def greet_across(peer, own_index):
        def one(q, c):
            @pl.when(jnp.logical_not(jnp.logical_and(own, q == own_index)))
            def _():
                pl.semaphore_signal(barrier, inc=1, device_id=peer(q), device_id_type=MESH)

            return c

        lax.fori_loop(0, M, one, 0)

    greet_across(target, own_target)
    greet_across(source, own_source)
    greet(ZH, zh, far_block)
    greet(M, m, near_chip)
    greet(N, rho, near_row)
    pl.semaphore_wait(barrier, 2 * M + (ZH - 1) + (M - 1) + (N - 1) - 2 * own.astype(jnp.int32))

    def spread(n, me, peer, src, dst, i):
        def one(t, c):
            p = lax.rem(me + t, n)
            pltpu.make_async_remote_copy(
                src_ref=src(p), dst_ref=dst.at[me], send_sem=send.at[i], recv_sem=recv.at[i],
                device_id=peer(p), device_id_type=MESH,
            ).start()
            return c

        lax.fori_loop(1, n, one, 0)
        pltpu.make_async_copy(src(me), dst.at[me], recv.at[i]).start()

    def arrived(dst, i):
        pltpu.make_async_copy(dst, dst, recv.at[i]).wait()

    def sent(dst, n, i):
        part = dst.at[pl.ds(0, n)]
        pltpu.make_async_copy(part, part, send.at[i]).wait()

    def across(peer, own_index, src, dst, slot, i):
        def one(q, c):
            mine = jnp.logical_and(own, q == own_index)

            @pl.when(mine)
            def _():
                pltpu.make_async_copy(src(q), dst.at[slot], recv.at[i]).start()

            @pl.when(jnp.logical_not(mine))
            def _():
                pltpu.make_async_remote_copy(
                    src_ref=src(q), dst_ref=dst.at[slot], send_sem=send.at[i], recv_sem=recv.at[i],
                    device_id=peer(q), device_id_type=MESH,
                ).start()

            return c

        lax.fori_loop(0, M, one, 0)

    def sent_across(dst, i):
        @pl.when(own)
        def _():
            sent(dst, M - 1, i)

        @pl.when(jnp.logical_not(own))
        def _():
            sent(dst, M, i)

    def columns(q):
        return a_ref.at[:, pl.ds(pl.multiple_of(q * LANES, LANES), LANES)]

    across(target, own_target, columns, ta, own_source, 0)
    spread(N, rho, near_row, lambda p: b_ref, pb, 1)

    def normalize(normed):
        values = xf[...]
        center = jnp.sum(values, 0, keepdims=True) / images
        shifted = values - center
        spread_ = jnp.sum(shifted * shifted, 0, keepdims=True) / images
        scaled = lax.rsqrt(spread_ + epsilon)
        normed[...] = (shifted * scaled).astype(bf16)
        return scaled

    own_rows = pl.ds(pl.multiple_of(rho * rows, rows), rows)

    def gram(normed, out):
        g = lax.dot_general(
            normed[own_rows, :], normed[...], (((1,), (1,)), ((), ())), preferred_element_type=f32
        )
        out[...] = g.reshape(M, SUB, images).astype(bf16)

    def summed(parts):
        return functools.reduce(jnp.add, [parts[i].astype(f32) for i in range(parts.shape[0])])

    arrived(pb, 1)
    low = lax.broadcasted_iota(jnp.int32, (rows, LANES), 1) < LANES // 2
    for i in range(R):
        p0, p1 = pb[2 * i].astype(f32), pb[2 * i + 1].astype(f32)
        xf[pl.ds(2 * i * rows, rows), :] = jnp.where(low, p0, pltpu.roll(p1, LANES // 2, 1))
        xf[pl.ds((2 * i + 1) * rows, rows), :] = jnp.where(low, pltpu.roll(p0, LANES // 2, 1), p1)
    scaled_b = normalize(nb)
    gram(nb, gp_b)
    spread(M, m, near_chip, lambda p: gp_b.at[p], ra_b, 2)

    arrived(ta, 0)
    spread(N, rho, near_row, lambda p: ta, xa, 3)

    arrived(ra_b, 2)
    hs_b[...] = summed(ra_b).astype(bf16)
    spread(ZH, zh, far_block, lambda p: hs_b, rb_b, 4)

    arrived(xa, 3)
    for i in range(N):
        xf[pl.ds(i * rows, rows), :] = xa[i].astype(f32).reshape(rows, LANES)
    scaled_a = normalize(na)
    gram(na, gp_a)
    spread(M, m, near_chip, lambda p: gp_a.at[p], ra_a, 5)

    corr = jnp.sum(na[...].astype(f32) * nb[...].astype(f32), 0, keepdims=True) / images
    d = 2.0 * (corr - 1.0) - (2.0 * off_weight) * corr
    ds0[...] = jnp.broadcast_to(jnp.square(1.0 - corr) - off_weight * jnp.square(corr), ds0.shape)
    spread(M, m, near_chip, lambda p: ds0, db0, 6)

    arrived(ra_a, 5)
    hs_a[...] = summed(ra_a).astype(bf16)
    spread(ZH, zh, far_block, lambda p: hs_a, rb_a, 7)

    arrived(db0, 6)
    ds1[...] = summed(db0)
    spread(ZH, zh, far_block, lambda p: ds1, db1, 8)

    arrived(rb_b, 4)
    ms_b[...] = summed(rb_b).astype(bf16)
    spread(M, m, near_chip, lambda p: ms_b, rg_b, 9)

    mine_a, mine_b = na[own_rows, :].astype(f32), nb[own_rows, :].astype(f32)
    line = lax.broadcasted_iota(jnp.int32, (SUB, LANES), 0)

    def term_of(rg, normed, other):
        g = rg[...].astype(f32).reshape(rows, images)
        product = jnp.dot(g.astype(bf16), normed[...], preferred_element_type=f32)
        return (2.0 * off_weight / images) * product + other * d, g

    def tile_of(*lines):
        out = jnp.zeros((SUB, LANES), f32)
        for i, v in enumerate(lines):
            out = jnp.where(line == i, jnp.broadcast_to(v, out.shape), out)
        return out

    def projected(term, mine, scaled, first, second):
        return scaled * (term - first / images - mine * (second / images))

    arrived(rg_b, 9)
    term_a, g_b = term_of(rg_b, na, mine_b)
    ss_a[...] = tile_of(jnp.sum(term_a, 0, keepdims=True), jnp.sum(term_a * mine_a, 0, keepdims=True))
    spread(N, rho, near_row, lambda p: ss_a, sb_a, 10)

    arrived(sb_a, 10)
    sums = summed(sb_a)
    grad_a = projected(term_a, mine_a, scaled_a, sums[0:1], sums[1:2])
    fs[...] = grad_a.reshape(M, SUB, LANES).astype(bf16)
    across(source, own_source, lambda b: fs.at[b], fa, own_target, 11)

    arrived(rb_a, 7)
    ms_a[...] = summed(rb_a).astype(bf16)
    spread(M, m, near_chip, lambda p: ms_a, rg_a, 12)
    arrived(rg_a, 12)
    term_b, g_a = term_of(rg_a, nb, mine_a)
    both = jnp.sum(g_a * g_b, 0, keepdims=True)
    trace = functools.reduce(jnp.add, [both[:, i * LANES : (i + 1) * LANES] for i in range(images // LANES)])
    ss_b[...] = tile_of(
        jnp.sum(term_b, 0, keepdims=True), jnp.sum(term_b * mine_b, 0, keepdims=True), trace
    )
    spread(N, rho, near_row, lambda p: ss_b, sb_b, 13)
    arrived(sb_b, 13)
    sums = summed(sb_b)
    grad_b = projected(term_b, mine_b, scaled_b, sums[0:1], sums[1:2])
    tb[...] = grad_b.astype(bf16)
    partner = pltpu.make_async_remote_copy(
        src_ref=tb, dst_ref=tp, send_sem=send.at[14], recv_sem=recv.at[14],
        device_id=device(r, z, yh, 1 - k), device_id_type=MESH,
    )
    partner.start()

    arrived(db1, 8)
    diagonal = summed(db1)[0:1]
    each = diagonal + sums[2:3] * (off_weight / (images * images))
    loss_ref[...] = jnp.broadcast_to(jnp.sum(each, 1, keepdims=True) / features, loss_ref.shape)

    partner.wait()
    other = tp[...].astype(f32)
    first_half = jnp.where(low, grad_b, pltpu.roll(other, LANES // 2, 1))
    second_half = jnp.where(low, pltpu.roll(other, LANES // 2, 1), grad_b)
    gb_ref[...] = jnp.where(k == 0, first_half, second_half).astype(bf16)

    arrived(fa, 11)
    for q in range(M):
        ga_ref[:, q * LANES : (q + 1) * LANES] = fa[q]

    sent_across(ta, 0)
    sent_across(fa, 11)
    for i, dst in ((1, pb), (3, xa), (10, sb_a), (13, sb_b)):
        sent(dst, N - 1, i)
    for i, dst in ((2, ra_b), (5, ra_a), (6, db0), (9, rg_b), (12, rg_a)):
        sent(dst, M - 1, i)
    for i, dst in ((4, rb_b), (7, rb_a), (8, db1)):
        sent(dst, ZH - 1, i)


def solution_on(split, interpret=False):
    YL, X, Z, YH, _ = split.devices.shape
    R = YL * X
    ZH, ZL = R, Z // R
    M, N = ZL * YH, R * K
    rows = M * SUB
    images = N * rows

    def body(view_a, view_b):
        packed = jnp.concatenate([view_b[:rows], view_b[rows:]], axis=1)
        vmem = pltpu.VMEM
        loss, grad_a, packed_b = pl.pallas_call(
            functools.partial(kernel, X, ZL, YH, ZH),
            out_shape=(
                jax.ShapeDtypeStruct((SUB, LANES), f32),
                jax.ShapeDtypeStruct(view_a.shape, bf16),
                jax.ShapeDtypeStruct(packed.shape, bf16),
            ),
            in_specs=[pl.BlockSpec(memory_space=pltpu.VMEM)] * 2,
            out_specs=[pl.BlockSpec(memory_space=pltpu.VMEM)] * 3,
            scratch_shapes=[
                vmem((M, SUB, LANES), bf16),
                vmem((N, M, SUB, LANES), bf16),
                vmem((N, rows, LANES), bf16),
                vmem((images, LANES), f32),
                vmem((images, LANES), bf16),
                vmem((images, LANES), bf16),
                vmem((M, SUB, images), bf16),
                vmem((M, SUB, images), bf16),
                vmem((M, SUB, images), bf16),
                vmem((M, SUB, images), bf16),
                vmem((SUB, images), bf16),
                vmem((SUB, images), bf16),
                vmem((ZH, SUB, images), bf16),
                vmem((ZH, SUB, images), bf16),
                vmem((SUB, images), bf16),
                vmem((SUB, images), bf16),
                vmem((M, SUB, images), bf16),
                vmem((M, SUB, images), bf16),
                vmem((SUB, LANES), f32),
                vmem((M, SUB, LANES), f32),
                vmem((SUB, LANES), f32),
                vmem((ZH, SUB, LANES), f32),
                vmem((SUB, LANES), f32),
                vmem((N, SUB, LANES), f32),
                vmem((SUB, LANES), f32),
                vmem((N, SUB, LANES), f32),
                vmem((M, SUB, LANES), bf16),
                vmem((M, SUB, LANES), bf16),
                vmem((rows, LANES), bf16),
                vmem((rows, LANES), bf16),
                pltpu.SemaphoreType.DMA((15,)),
                pltpu.SemaphoreType.DMA((15,)),
            ],
            compiler_params=pltpu.CompilerParams(collective_id=0, has_side_effects=True),
            interpret=interpret,
        )(view_a, packed)
        half = LANES // K
        grad_b = jnp.concatenate([packed_b[:, :half], packed_b[:, half:]], axis=0)
        return loss[0, 0], grad_a, grad_b

    return jax.shard_map(
        body,
        mesh=split,
        in_specs=(P(COL, ROW), P(ROW, COL)),
        out_specs=(P(), P(COL, ROW), P(ROW, COL)),
        check_vma=False,
    )


def solution(mesh):
    return solution_on(Mesh(mesh.devices.reshape(2, 4, 32, 2, 2), AXES))
```

```python
import functools

import jax
import jax.numpy as jnp
from jax import lax
from jax.experimental import pallas as pl
from jax.experimental.pallas import tpu as pltpu
from jax.sharding import Mesh
from jax.sharding import PartitionSpec as P

AXES = ("yl", "x", "z", "yh", "k")
ROW = ("yl", "x")
COL = ("z", "yh", "k")
MESH = pl.DeviceIdType.MESH

off_weight = 0.0051
epsilon = 1e-05
K = 2
LANES = 128
SUB = 8

f32 = jnp.float32
bf16 = jnp.bfloat16


def kernel(
    X, ZL, YH, ZH,
    a_ref, view_ref, loss_ref, ga_ref, gb_ref,
    b_ref, ta, xa, pb, xf, na, nb,
    gp_a, gp_b, ra_a, ra_b, hs_a, hs_b, rb_a, rb_b, ms_a, ms_b, rg_a, rg_b,
    ds0, db0, ds1, db1, ss_a, sb_a, ss_b, sb_b, fs, fa, tb, tp,
    send, recv, ring, hop,
):
    R, M = ZH, ZL * YH
    N = R * K
    rows = M * SUB
    images = N * rows
    features = ZH * M * LANES
    yl, x, z, yh, k = (lax.axis_index(name) for name in AXES)
    r = yl * X + x
    zh, zl = z // ZL, z % ZL
    rho, m = r * K + k, zl * YH + yh
    s = m * K + k

    def device(r_, z_, yh_, k_):
        return (r_ // X, r_ % X, z_, yh_, k_)

    def near_row(p):
        return device(p // K, z, yh, p % K)

    def near_chip(p):
        return device(r, zh * ZL + p // YH, p % YH, k)

    def far_block(p):
        return device(r, p * ZL + zl, yh, k)

    def target(q):
        return device(zh, r * ZL + q // YH, q % YH, s // M)

    def source(b):
        s_ = k * M + b
        return device(zh, r * ZL + (s_ // K) // YH, (s_ // K) % YH, s_ % K)

    own = jnp.logical_and(zh == r, s // M == k)
    own_target, own_source = m, s % M

    half = LANES // K
    view_b = view_ref[...].astype(f32).T
    b_ref[...] = jnp.concatenate([view_b[:rows], view_b[rows:]], axis=1).astype(bf16)

    barrier = pltpu.get_barrier_semaphore()

    def greet(n, me, peer):
        def one(t, c):
            pl.semaphore_signal(barrier, inc=1, device_id=peer(lax.rem(me + t, n)), device_id_type=MESH)
            return c

        lax.fori_loop(1, n, one, 0)

    def greet_across(peer, own_index):
        def one(q, c):
            @pl.when(jnp.logical_not(jnp.logical_and(own, q == own_index)))
            def _():
                pl.semaphore_signal(barrier, inc=1, device_id=peer(q), device_id_type=MESH)

            return c

        lax.fori_loop(0, M, one, 0)

    greet_across(target, own_target)
    greet_across(source, own_source)
    greet(ZH, zh, far_block)
    greet(M, m, near_chip)
    greet(N, rho, near_row)
    with jax.named_scope("s0_barrier"):
        pl.semaphore_wait(barrier, 2 * M + (ZH - 1) + (M - 1) + (N - 1) - 2 * own.astype(jnp.int32))

    def spread(n, me, peer, src, dst, i):
        def one(t, c):
            p = lax.rem(me + t, n)
            pltpu.make_async_remote_copy(
                src_ref=src(p), dst_ref=dst.at[me], send_sem=send.at[i], recv_sem=recv.at[i],
                device_id=peer(p), device_id_type=MESH,
            ).start()
            return c

        lax.fori_loop(1, n, one, 0)
        pltpu.make_async_copy(src(me), dst.at[me], recv.at[i]).start()

    def arrived(dst, i):
        with jax.named_scope(f"w{i}"):
            pltpu.make_async_copy(dst, dst, recv.at[i]).wait()

    def sent(dst, n, i):
        part = dst.at[pl.ds(0, n)]
        pltpu.make_async_copy(part, part, send.at[i]).wait()

    def across(peer, own_index, src, dst, slot, i):
        def one(q, c):
            mine = jnp.logical_and(own, q == own_index)

            @pl.when(mine)
            def _():
                pltpu.make_async_copy(src(q), dst.at[slot], recv.at[i]).start()

            @pl.when(jnp.logical_not(mine))
            def _():
                pltpu.make_async_remote_copy(
                    src_ref=src(q), dst_ref=dst.at[slot], send_sem=send.at[i], recv_sem=recv.at[i],
                    device_id=peer(q), device_id_type=MESH,
                ).start()

            return c

        lax.fori_loop(0, M, one, 0)

    def sent_across(dst, i):
        @pl.when(own)
        def _():
            sent(dst, M - 1, i)

        @pl.when(jnp.logical_not(own))
        def _():
            sent(dst, M, i)

    up, down = ZH // 2, ZH - 1 - ZH // 2

    def pass_on(src, dst, slot, i, j, step):
        pltpu.make_async_remote_copy(
            src_ref=src, dst_ref=dst.at[slot], send_sem=ring.at[i], recv_sem=hop.at[i, j],
            device_id=far_block(lax.rem(zh + step + ZH, ZH)), device_id_type=MESH,
        ).start()

    def came(dst, slot, i, j):
        with jax.named_scope(f"h{i}_{j}"):
            pltpu.make_async_copy(dst.at[slot], dst.at[slot], hop.at[i, j]).wait()

    def ring_start(src, dst, i):
        pltpu.make_async_copy(src, dst.at[zh], hop.at[i, 0]).start()
        pass_on(src, dst, zh, i, 1, 1)
        if down:
            pass_on(src, dst, zh, i, up + 1, -1)

    def ring_step(dst, i, j):
        if j <= up:
            slot = lax.rem(zh - j + ZH, ZH)
            came(dst, slot, i, j)
            if j < up:
                pass_on(dst.at[slot], dst, slot, i, j + 1, 1)
        if j <= down:
            slot = lax.rem(zh + j, ZH)
            came(dst, slot, i, up + j)
            if j < down:
                pass_on(dst.at[slot], dst, slot, i, up + j + 1, -1)
        if j == up:
            came(dst, zh, i, 0)

    def columns(q):
        return a_ref.at[:, pl.ds(pl.multiple_of(q * LANES, LANES), LANES)]

    across(target, own_target, columns, ta, own_source, 0)
    spread(N, rho, near_row, lambda p: b_ref, pb, 1)

    def normalize(normed):
        values = xf[...]
        center = jnp.sum(values, 0, keepdims=True) / images
        shifted = values - center
        spread_ = jnp.sum(shifted * shifted, 0, keepdims=True) / images
        scaled = lax.rsqrt(spread_ + epsilon)
        normed[...] = (shifted * scaled).astype(bf16)
        return scaled

    own_rows = pl.ds(pl.multiple_of(rho * rows, rows), rows)

    def gram(normed, out):
        g = lax.dot_general(
            normed[own_rows, :], normed[...], (((1,), (1,)), ((), ())), preferred_element_type=f32
        )
        out[...] = g.reshape(M, SUB, images).astype(bf16)

    def summed(parts):
        return functools.reduce(jnp.add, [parts[i].astype(f32) for i in range(parts.shape[0])])

    arrived(pb, 1)
    low = lax.broadcasted_iota(jnp.int32, (rows, LANES), 1) < LANES // 2
    for i in range(R):
        p0, p1 = pb[2 * i].astype(f32), pb[2 * i + 1].astype(f32)
        xf[pl.ds(2 * i * rows, rows), :] = jnp.where(low, p0, pltpu.roll(p1, LANES // 2, 1))
        xf[pl.ds((2 * i + 1) * rows, rows), :] = jnp.where(low, pltpu.roll(p0, LANES // 2, 1), p1)
    scaled_b = normalize(nb)
    gram(nb, gp_b)
    spread(M, m, near_chip, lambda p: gp_b.at[p], ra_b, 2)

    arrived(ra_b, 2)
    hs_b[...] = summed(ra_b).astype(bf16)
    ring_start(hs_b, rb_b, 0)

    arrived(ta, 0)
    spread(N, rho, near_row, lambda p: ta, xa, 3)
    for j in range(1, up):
        ring_step(rb_b, 0, j)

    arrived(xa, 3)
    for i in range(N):
        xf[pl.ds(i * rows, rows), :] = xa[i].astype(f32).reshape(rows, LANES)
    scaled_a = normalize(na)
    gram(na, gp_a)
    spread(M, m, near_chip, lambda p: gp_a.at[p], ra_a, 5)

    corr = jnp.sum(na[...].astype(f32) * nb[...].astype(f32), 0, keepdims=True) / images
    d = 2.0 * (corr - 1.0) - (2.0 * off_weight) * corr
    ds0[...] = jnp.broadcast_to(jnp.square(1.0 - corr) - off_weight * jnp.square(corr), ds0.shape)
    spread(M, m, near_chip, lambda p: ds0, db0, 6)

    arrived(ra_a, 5)
    hs_a[...] = summed(ra_a).astype(bf16)
    ring_start(hs_a, rb_a, 1)

    ring_step(rb_b, 0, up)
    ms_b[...] = summed(rb_b).astype(bf16)
    spread(M, m, near_chip, lambda p: ms_b, rg_b, 9)

    arrived(db0, 6)
    ds1[...] = summed(db0)
    spread(ZH, zh, far_block, lambda p: ds1, db1, 8)

    mine_a, mine_b = na[own_rows, :].astype(f32), nb[own_rows, :].astype(f32)
    line = lax.broadcasted_iota(jnp.int32, (SUB, LANES), 0)
    if up > 1:
        ring_step(rb_a, 1, 1)

    def term_of(rg, normed, other):
        g = rg[...].astype(f32).reshape(rows, images)
        product = jnp.dot(g.astype(bf16), normed[...], preferred_element_type=f32)
        return (2.0 * off_weight / images) * product + other * d, g

    def tile_of(*lines):
        out = jnp.zeros((SUB, LANES), f32)
        for i, v in enumerate(lines):
            out = jnp.where(line == i, jnp.broadcast_to(v, out.shape), out)
        return out

    def projected(term, mine, scaled, first, second):
        return scaled * (term - first / images - mine * (second / images))

    arrived(rg_b, 9)
    term_a, g_b = term_of(rg_b, na, mine_b)
    ss_a[...] = tile_of(jnp.sum(term_a, 0, keepdims=True), jnp.sum(term_a * mine_a, 0, keepdims=True))
    spread(N, rho, near_row, lambda p: ss_a, sb_a, 10)

    for j in range(2, up - 1):
        ring_step(rb_a, 1, j)

    arrived(sb_a, 10)
    sums = summed(sb_a)
    grad_a = projected(term_a, mine_a, scaled_a, sums[0:1], sums[1:2])
    fs[...] = grad_a.reshape(M, SUB, LANES).astype(bf16)
    across(source, own_source, lambda b: fs.at[b], fa, own_target, 11)

    for j in range(max(up - 1, 2), up):
        ring_step(rb_a, 1, j)
    ring_step(rb_a, 1, up)
    ms_a[...] = summed(rb_a).astype(bf16)
    spread(M, m, near_chip, lambda p: ms_a, rg_a, 12)
    arrived(rg_a, 12)
    term_b, g_a = term_of(rg_a, nb, mine_a)
    both = jnp.sum(g_a * g_b, 0, keepdims=True)
    trace = functools.reduce(jnp.add, [both[:, i * LANES : (i + 1) * LANES] for i in range(images // LANES)])
    ss_b[...] = tile_of(
        jnp.sum(term_b, 0, keepdims=True), jnp.sum(term_b * mine_b, 0, keepdims=True), trace
    )
    spread(N, rho, near_row, lambda p: ss_b, sb_b, 13)
    arrived(sb_b, 13)
    sums = summed(sb_b)
    grad_b = projected(term_b, mine_b, scaled_b, sums[0:1], sums[1:2])
    tb[...] = grad_b.astype(bf16)
    partner = pltpu.make_async_remote_copy(
        src_ref=tb, dst_ref=tp, send_sem=send.at[14], recv_sem=recv.at[14],
        device_id=device(r, z, yh, 1 - k), device_id_type=MESH,
    )
    partner.start()

    arrived(db1, 8)
    diagonal = summed(db1)[0:1]
    each = diagonal + sums[2:3] * (off_weight / (images * images))
    loss_ref[0, 0] = jnp.sum(each) / features

    with jax.named_scope("w14"):
        partner.wait()
    other = tp[...].astype(f32)
    turned, other_turned = pltpu.roll(grad_b, half, 1), pltpu.roll(other, half, 1)
    gb_ref[:rows, :] = jnp.where(k == 0, grad_b, other_turned)[:, :half].astype(bf16)
    gb_ref[rows:, :] = jnp.where(k == 0, other, turned)[:, :half].astype(bf16)

    arrived(fa, 11)
    for q in range(M):
        ga_ref[:, q * LANES : (q + 1) * LANES] = fa[q]

    sent_across(ta, 0)
    sent_across(fa, 11)
    for i, dst in ((1, pb), (3, xa), (10, sb_a), (13, sb_b)):
        sent(dst, N - 1, i)
    for i, dst in ((2, ra_b), (5, ra_a), (6, db0), (9, rg_b), (12, rg_a)):
        sent(dst, M - 1, i)
    for i, dst in ((0, rb_b), (1, rb_a)):
        part = dst.at[pl.ds(0, ZH - 1)]
        pltpu.make_async_copy(part, part, ring.at[i]).wait()
    sent(db1, ZH - 1, 8)


def solution_on(split, interpret=False):
    YL, X, Z, YH, _ = split.devices.shape
    R = YL * X
    ZH, ZL = R, Z // R
    M, N = ZL * YH, R * K
    rows = M * SUB
    images = N * rows

    def body(view_a, view_b):
        vmem = pltpu.VMEM
        loss, grad_a, grad_b = pl.pallas_call(
            functools.partial(kernel, X, ZL, YH, ZH),
            out_shape=(
                jax.ShapeDtypeStruct((1, 1), f32),
                jax.ShapeDtypeStruct(view_a.shape, bf16),
                jax.ShapeDtypeStruct(view_b.shape, bf16),
            ),
            in_specs=[pl.BlockSpec(memory_space=pltpu.VMEM)] * 2,
            out_specs=[
                pl.BlockSpec(memory_space=pltpu.SMEM),
                pl.BlockSpec(memory_space=pltpu.VMEM),
                pl.BlockSpec(memory_space=pltpu.VMEM),
            ],
            scratch_shapes=[
                vmem((rows, LANES), bf16),
                vmem((M, SUB, LANES), bf16),
                vmem((N, M, SUB, LANES), bf16),
                vmem((N, rows, LANES), bf16),
                vmem((images, LANES), f32),
                vmem((images, LANES), bf16),
                vmem((images, LANES), bf16),
                vmem((M, SUB, images), bf16),
                vmem((M, SUB, images), bf16),
                vmem((M, SUB, images), bf16),
                vmem((M, SUB, images), bf16),
                vmem((SUB, images), bf16),
                vmem((SUB, images), bf16),
                vmem((ZH, SUB, images), bf16),
                vmem((ZH, SUB, images), bf16),
                vmem((SUB, images), bf16),
                vmem((SUB, images), bf16),
                vmem((M, SUB, images), bf16),
                vmem((M, SUB, images), bf16),
                vmem((SUB, LANES), f32),
                vmem((M, SUB, LANES), f32),
                vmem((SUB, LANES), f32),
                vmem((ZH, SUB, LANES), f32),
                vmem((SUB, LANES), f32),
                vmem((N, SUB, LANES), f32),
                vmem((SUB, LANES), f32),
                vmem((N, SUB, LANES), f32),
                vmem((M, SUB, LANES), bf16),
                vmem((M, SUB, LANES), bf16),
                vmem((rows, LANES), bf16),
                vmem((rows, LANES), bf16),
                pltpu.SemaphoreType.DMA((15,)),
                pltpu.SemaphoreType.DMA((15,)),
                pltpu.SemaphoreType.DMA((2,)),
                pltpu.SemaphoreType.DMA((2, ZH)),
            ],
            compiler_params=pltpu.CompilerParams(collective_id=0, has_side_effects=True),
            interpret=interpret,
        )(view_a, view_b.T)
        return loss.reshape(()), grad_a, grad_b

    return jax.shard_map(
        body,
        mesh=split,
        in_specs=(P(COL, ROW), P(ROW, COL)),
        out_specs=(P(), P(COL, ROW), P(ROW, COL)),
        check_vma=False,
    )


def solution(mesh):
    return solution_on(Mesh(mesh.devices.reshape(2, 4, 32, 2, 2), AXES))
```

```python
import functools

import jax
import jax.numpy as jnp
from jax import lax
from jax.experimental import pallas as pl
from jax.experimental.pallas import tpu as pltpu
from jax.sharding import Mesh
from jax.sharding import PartitionSpec as P

AXES = ("yl", "x", "z", "yh", "k")
ROW = ("yl", "x")
COL = ("z", "yh", "k")
MESH = pl.DeviceIdType.MESH

off_weight = 0.0051
epsilon = 1e-05
K = 2
LANES = 128
SUB = 8

f32 = jnp.float32
bf16 = jnp.bfloat16


def kernel(
    X, ZL, YH, ZH,
    a_ref, view_ref, loss_ref, ga_ref, gb_ref,
    a_in, view_in, b_ref, ta, xa, pb, xf, na, nb,
    gp_a, gp_b, ra_a, ra_b, hs_a, hs_b, rb_a, rb_b, ms_a, ms_b, rg_a, rg_b,
    ss_a, sb_a, ss_b, sb_b, ls, lb, fs, fa, tb, tp,
    send, recv, ring, hop,
):
    R, M = ZH, ZL * YH
    N = R * K
    rows = M * SUB
    images = N * rows
    features = ZH * M * LANES
    yl, x, z, yh, k = (lax.axis_index(name) for name in AXES)
    r = yl * X + x
    zh, zl = z // ZL, z % ZL
    rho, m = r * K + k, zl * YH + yh
    s = m * K + k

    def device(r_, z_, yh_, k_):
        return (r_ // X, r_ % X, z_, yh_, k_)

    def near_row(p):
        return device(p // K, z, yh, p % K)

    def near_chip(p):
        return device(r, zh * ZL + p // YH, p % YH, k)

    def far_block(p):
        return device(r, p * ZL + zl, yh, k)

    def target(q):
        return device(zh, r * ZL + q // YH, q % YH, s // M)

    def source(b):
        s_ = k * M + b
        return device(zh, r * ZL + (s_ // K) // YH, (s_ // K) % YH, s_ % K)

    own = jnp.logical_and(zh == r, s // M == k)
    own_target, own_source = m, s % M

    half = LANES // K
    fetch_a = pltpu.make_async_copy(a_ref, a_in, recv.at[6])
    fetch_b = pltpu.make_async_copy(view_ref, view_in, recv.at[7])
    fetch_a.start()
    fetch_b.start()

    barrier = pltpu.get_barrier_semaphore()

    def greet(n, me, peer):
        def one(t, c):
            pl.semaphore_signal(barrier, inc=1, device_id=peer(lax.rem(me + t, n)), device_id_type=MESH)
            return c

        lax.fori_loop(1, n, one, 0)

    def greet_across(peer, own_index):
        def one(q, c):
            @pl.when(jnp.logical_not(jnp.logical_and(own, q == own_index)))
            def _():
                pl.semaphore_signal(barrier, inc=1, device_id=peer(q), device_id_type=MESH)

            return c

        lax.fori_loop(0, M, one, 0)

    greet_across(target, own_target)
    greet_across(source, own_source)
    for step in (1, ZH - 1)[: ZH - 1]:
        pl.semaphore_signal(barrier, inc=1, device_id=far_block(lax.rem(zh + step, ZH)), device_id_type=MESH)
    greet(M, m, near_chip)
    greet(N, rho, near_row)
    fetch_b.wait()
    view_b = view_in[...].astype(f32).T
    b_ref[...] = jnp.concatenate([view_b[:rows], view_b[rows:]], axis=1).astype(bf16)
    fetch_a.wait()
    with jax.named_scope("s0_barrier"):
        pl.semaphore_wait(barrier, 2 * M + min(ZH - 1, 2) + (M - 1) + (N - 1) - 2 * own.astype(jnp.int32))

    def spread(n, me, peer, src, dst, i):
        def one(t, c):
            p = lax.rem(me + t, n)
            pltpu.make_async_remote_copy(
                src_ref=src(p), dst_ref=dst.at[me], send_sem=send.at[i], recv_sem=recv.at[i],
                device_id=peer(p), device_id_type=MESH,
            ).start()
            return c

        lax.fori_loop(1, n, one, 0)
        pltpu.make_async_copy(src(me), dst.at[me], recv.at[i]).start()

    def arrived(dst, i):
        with jax.named_scope(f"w{i}"):
            pltpu.make_async_copy(dst, dst, recv.at[i]).wait()

    def sent(dst, n, i):
        part = dst.at[pl.ds(0, n)]
        pltpu.make_async_copy(part, part, send.at[i]).wait()

    def across(peer, own_index, src, dst, slot, i):
        def one(q, c):
            mine = jnp.logical_and(own, q == own_index)

            @pl.when(mine)
            def _():
                pltpu.make_async_copy(src(q), dst.at[slot], recv.at[i]).start()

            @pl.when(jnp.logical_not(mine))
            def _():
                pltpu.make_async_remote_copy(
                    src_ref=src(q), dst_ref=dst.at[slot], send_sem=send.at[i], recv_sem=recv.at[i],
                    device_id=peer(q), device_id_type=MESH,
                ).start()

            return c

        lax.fori_loop(0, M, one, 0)

    def sent_across(dst, i):
        @pl.when(own)
        def _():
            sent(dst, M - 1, i)

        @pl.when(jnp.logical_not(own))
        def _():
            sent(dst, M, i)

    up, down = ZH // 2, ZH - 1 - ZH // 2

    def pass_on(src, dst, slot, i, j, step):
        pltpu.make_async_remote_copy(
            src_ref=src, dst_ref=dst.at[slot], send_sem=ring.at[i], recv_sem=hop.at[i, j],
            device_id=far_block(lax.rem(zh + step + ZH, ZH)), device_id_type=MESH,
        ).start()

    def came(dst, slot, i, j):
        with jax.named_scope(f"h{i}_{j}"):
            pltpu.make_async_copy(dst.at[slot], dst.at[slot], hop.at[i, j]).wait()

    def ring_start(src, dst, i):
        pltpu.make_async_copy(src, dst.at[zh], hop.at[i, 0]).start()
        pass_on(src, dst, zh, i, 1, 1)
        if down:
            pass_on(src, dst, zh, i, up + 1, -1)

    def ring_step(dst, i, j):
        if j <= up:
            slot = lax.rem(zh - j + ZH, ZH)
            came(dst, slot, i, j)
            if j < up:
                pass_on(dst.at[slot], dst, slot, i, j + 1, 1)
        if j <= down:
            slot = lax.rem(zh + j, ZH)
            came(dst, slot, i, up + j)
            if j < down:
                pass_on(dst.at[slot], dst, slot, i, up + j + 1, -1)
        if j == up:
            came(dst, zh, i, 0)

    def columns(q):
        return a_in.at[:, pl.ds(pl.multiple_of(q * LANES, LANES), LANES)]

    across(target, own_target, columns, ta, own_source, 0)
    spread(N, rho, near_row, lambda p: b_ref, pb, 1)

    def normalize(normed):
        values = xf[...]
        center = jnp.sum(values, 0, keepdims=True) / images
        shifted = values - center
        spread_ = jnp.sum(shifted * shifted, 0, keepdims=True) / images
        scaled = lax.rsqrt(spread_ + epsilon)
        normed[...] = (shifted * scaled).astype(bf16)
        return scaled

    own_rows = pl.ds(pl.multiple_of(rho * rows, rows), rows)

    def gram(normed, out):
        g = lax.dot_general(
            normed[own_rows, :], normed[...], (((1,), (1,)), ((), ())), preferred_element_type=f32
        )
        out[:, :, :images] = g.reshape(M, SUB, images).astype(bf16)

    def parts_of(v):
        high = v.astype(bf16).astype(f32)
        middle = (v - high).astype(bf16).astype(f32)
        return tile_of(high, middle, v - high - middle).astype(bf16)

    def summed(parts):
        return functools.reduce(jnp.add, [parts[i].astype(f32) for i in range(parts.shape[0])])

    line = lax.broadcasted_iota(jnp.int32, (SUB, LANES), 0)

    def term_of(rg, normed, other):
        g = rg[...].astype(f32).reshape(rows, images)
        product = jnp.dot(g.astype(bf16), normed[...], preferred_element_type=f32)
        return (2.0 * off_weight / images) * product + other * d, g

    def tile_of(*lines):
        out = jnp.zeros((SUB, LANES), f32)
        for i, v in enumerate(lines):
            out = jnp.where(line == i, jnp.broadcast_to(v, out.shape), out)
        return out

    def projected(term, mine, scaled, first, second):
        return scaled * (term - first / images - mine * (second / images))

    arrived(pb, 1)
    low = lax.broadcasted_iota(jnp.int32, (rows, LANES), 1) < half
    for i in range(R):
        p0, p1 = pb[2 * i].astype(f32), pb[2 * i + 1].astype(f32)
        xf[pl.ds(2 * i * rows, rows), :] = jnp.where(low, p0, pltpu.roll(p1, half, 1))
        xf[pl.ds((2 * i + 1) * rows, rows), :] = jnp.where(low, pltpu.roll(p0, half, 1), p1)
    scaled_b = normalize(nb)
    gram(nb, gp_b)
    spread(M, m, near_chip, lambda p: gp_b.at[p], ra_b, 2)

    arrived(ta, 0)
    spread(N, rho, near_row, lambda p: ta, xa, 3)

    arrived(ra_b, 2)
    hs_b[...] = summed(ra_b).astype(bf16)
    ring_start(hs_b, rb_b, 0)

    arrived(xa, 3)
    for i in range(N):
        xf[pl.ds(i * rows, rows), :] = xa[i].astype(f32).reshape(rows, LANES)
    scaled_a = normalize(na)
    gram(na, gp_a)
    corr = jnp.sum(na[...].astype(f32) * nb[...].astype(f32), 0, keepdims=True) / images
    d = 2.0 * (corr - 1.0) - (2.0 * off_weight) * corr
    parts = parts_of(jnp.square(1.0 - corr) - off_weight * jnp.square(corr))
    for i in range(M):
        gp_a[i, :, images:] = parts
    spread(M, m, near_chip, lambda p: gp_a.at[p], ra_a, 4)
    mine_a, mine_b = na[own_rows, :].astype(f32), nb[own_rows, :].astype(f32)
    if up > 1:
        ring_step(rb_b, 0, 1)

    arrived(ra_a, 4)
    near = summed(ra_a)
    hs_a[:, :images] = near[:, :images].astype(bf16)
    hs_a[:, images:] = parts_of(jnp.sum(near[:, images:], 0, keepdims=True))
    ring_start(hs_a, rb_a, 1)

    for j in range(2, up):
        ring_step(rb_b, 0, j)
    if up > 1:
        ring_step(rb_a, 1, 1)
    ring_step(rb_b, 0, up)
    ms_b[...] = summed(rb_b).astype(bf16)
    spread(M, m, near_chip, lambda p: ms_b, rg_b, 9)
    if up > 2:
        ring_step(rb_a, 1, 2)

    arrived(rg_b, 9)
    term_a, g_b = term_of(rg_b, na, mine_b)
    ss_a[...] = tile_of(jnp.sum(term_a, 0, keepdims=True), jnp.sum(term_a * mine_a, 0, keepdims=True))
    spread(N, rho, near_row, lambda p: ss_a, sb_a, 10)
    for j in range(3, up):
        ring_step(rb_a, 1, j)

    arrived(sb_a, 10)
    sums = summed(sb_a)
    grad_a = projected(term_a, mine_a, scaled_a, sums[0:1], sums[1:2])
    fs[...] = grad_a.reshape(M, SUB, LANES).astype(bf16)
    across(source, own_source, lambda b: fs.at[b], fa, own_target, 11)

    ring_step(rb_a, 1, up)
    whole = summed(rb_a)
    ms_a[...] = whole[:, :images].astype(bf16)
    spread(M, m, near_chip, lambda p: ms_a, rg_a, 12)
    diagonal = jnp.sum(whole[:, images:], 0, keepdims=True)

    arrived(rg_a, 12)
    term_b, g_a = term_of(rg_a, nb, mine_a)
    tb[...] = term_b
    partner = pltpu.make_async_remote_copy(
        src_ref=tb, dst_ref=tp, send_sem=send.at[14], recv_sem=recv.at[14],
        device_id=device(r, z, yh, 1 - k), device_id_type=MESH,
    )
    partner.start()
    ss_b[...] = tile_of(jnp.sum(term_b, 0, keepdims=True), jnp.sum(term_b * mine_b, 0, keepdims=True))
    spread(N, rho, near_row, lambda p: ss_b, sb_b, 13)
    both = jnp.sum(g_a * g_b, 0, keepdims=True)
    trace = functools.reduce(jnp.add, [both[:, i * LANES : (i + 1) * LANES] for i in range(images // LANES)])
    ls[...] = jnp.broadcast_to(trace, ls.shape)
    spread(N, rho, near_row, lambda p: ls, lb, 8)

    other_rows = pl.ds(pl.multiple_of((r * K + 1 - k) * rows, rows), rows)
    with jax.named_scope("w14"):
        partner.wait()
    other_b, other_mine = tp[...], nb[other_rows, :].astype(f32)
    arrived(sb_b, 13)
    sums = summed(sb_b)
    pieces = [
        projected(term, mine, scaled_b, sums[0:1], sums[1:2]).T
        for term, mine in ((term_b, mine_b), (other_b, other_mine))
    ]
    own_t, other_t = (jnp.where(k == 0, v[:half], v[half:]) for v in pieces)
    gb_ref[...] = jnp.where(
        k == 0, jnp.concatenate([own_t, other_t], axis=1), jnp.concatenate([other_t, own_t], axis=1)
    ).astype(bf16)

    arrived(lb, 8)
    each = diagonal + summed(lb)[0:1] * (off_weight / (images * images))
    loss_ref[0, 0] = jnp.sum(each) / features

    arrived(fa, 11)
    for q in range(M):
        ga_ref[:, q * LANES : (q + 1) * LANES] = fa[q]

    sent_across(ta, 0)
    sent_across(fa, 11)
    for i, dst in ((1, pb), (3, xa), (8, lb), (10, sb_a), (13, sb_b)):
        sent(dst, N - 1, i)
    for i, dst in ((2, ra_b), (4, ra_a), (9, rg_b), (12, rg_a)):
        sent(dst, M - 1, i)
    for i, dst in ((0, rb_b), (1, rb_a)):
        part = dst.at[pl.ds(0, ZH - 1)]
        pltpu.make_async_copy(part, part, ring.at[i]).wait()


def hand_over(loss_in, ga_in, gb_in, loss_ref, ga_ref, gb_ref):
    loss_ref[0, 0] = loss_in[0, 0]
    ga_ref[...] = ga_in[...]
    gb_ref[...] = gb_in[...]


def solution_on(split, interpret=False):
    YL, X, Z, YH, _ = split.devices.shape
    R = YL * X
    ZH, ZL = R, Z // R
    M, N = ZL * YH, R * K
    rows = M * SUB
    images = N * rows

    def body(view_a, view_b):
        vmem = pltpu.VMEM
        places = [pl.BlockSpec(memory_space=space) for space in (pltpu.SMEM, pltpu.VMEM, pltpu.VMEM)]
        loss, grad_a, grad_b = pl.pallas_call(
            functools.partial(kernel, X, ZL, YH, ZH),
            out_shape=(
                jax.ShapeDtypeStruct((1, 1), f32),
                jax.ShapeDtypeStruct(view_a.shape, bf16),
                jax.ShapeDtypeStruct(view_b.shape[::-1], bf16),
            ),
            in_specs=[pl.BlockSpec(memory_space=pl.ANY)] * 2,
            out_specs=places,
            scratch_shapes=[
                vmem(view_a.shape, bf16),
                vmem(view_b.shape[::-1], bf16),
                vmem((rows, LANES), bf16),
                vmem((M, SUB, LANES), bf16),
                vmem((N, M, SUB, LANES), bf16),
                vmem((N, rows, LANES), bf16),
                vmem((images, LANES), f32),
                vmem((images, LANES), bf16),
                vmem((images, LANES), bf16),
                vmem((M, SUB, images + LANES), bf16),
                vmem((M, SUB, images), bf16),
                vmem((M, SUB, images + LANES), bf16),
                vmem((M, SUB, images), bf16),
                vmem((SUB, images + LANES), bf16),
                vmem((SUB, images), bf16),
                vmem((ZH, SUB, images + LANES), bf16),
                vmem((ZH, SUB, images), bf16),
                vmem((SUB, images), bf16),
                vmem((SUB, images), bf16),
                vmem((M, SUB, images), bf16),
                vmem((M, SUB, images), bf16),
                vmem((SUB, LANES), f32),
                vmem((N, SUB, LANES), f32),
                vmem((SUB, LANES), f32),
                vmem((N, SUB, LANES), f32),
                vmem((SUB, LANES), f32),
                vmem((N, SUB, LANES), f32),
                vmem((M, SUB, LANES), bf16),
                vmem((M, SUB, LANES), bf16),
                vmem((rows, LANES), f32),
                vmem((rows, LANES), f32),
                pltpu.SemaphoreType.DMA((15,)),
                pltpu.SemaphoreType.DMA((15,)),
                pltpu.SemaphoreType.DMA((2,)),
                pltpu.SemaphoreType.DMA((2, ZH)),
            ],
            compiler_params=pltpu.CompilerParams(collective_id=0, has_side_effects=True),
            interpret=interpret,
        )(view_a, view_b.T)
        shapes = [jax.ShapeDtypeStruct(v.shape, v.dtype) for v in (loss, grad_a, grad_b)]
        loss, grad_a, grad_b = pl.pallas_call(
            hand_over, out_shape=shapes, in_specs=places, out_specs=places, interpret=interpret
        )(loss, grad_a, grad_b)
        return loss.reshape(()), grad_a, grad_b.T

    return jax.shard_map(
        body,
        mesh=split,
        in_specs=(P(COL, ROW), P(ROW, COL)),
        out_specs=(P(), P(COL, ROW), P(ROW, COL)),
        check_vma=False,
    )


def solution(mesh):
    return solution_on(Mesh(mesh.devices.reshape(2, 4, 32, 2, 2), AXES))
```

```python
import functools

import jax
import jax.numpy as jnp
from jax import lax
from jax.experimental import pallas as pl
from jax.experimental.pallas import tpu as pltpu
from jax.sharding import Mesh
from jax.sharding import PartitionSpec as P

AXES = ("yl", "x", "z", "yh", "k")
ROW = ("yl", "x")
COL = ("z", "yh", "k")
MESH = pl.DeviceIdType.MESH

off_weight = 0.0051
epsilon = 1e-05
K = 2
LANES = 128
SUB = 8

f32 = jnp.float32
bf16 = jnp.bfloat16


def kernel(
    X, ZL, YH, ZH,
    a_ref, view_ref, loss_ref, ga_ref, gb_ref,
    a_in, view_in, b_ref, ta, xa, pb, xf, na, nb,
    gp_a, gp_b, ra_a, ra_b, hs_a, hs_b, rb_a, rb_b, ms_a, ms_b, rg_a, rg_b,
    ss_a, sb_a, ss_b, sb_b, ls, lb, fs, fa, tb, tp,
    send, recv, ring, hop,
):
    R, M = ZH, ZL * YH
    N = R * K
    rows = M * SUB
    images = N * rows
    features = ZH * M * LANES
    yl, x, z, yh, k = (lax.axis_index(name) for name in AXES)
    r = yl * X + x
    zh, zl = z // ZL, z % ZL
    rho, m = r * K + k, zl * YH + yh
    s = m * K + k

    def device(r_, z_, yh_, k_):
        return (r_ // X, r_ % X, z_, yh_, k_)

    def near_row(p):
        return device(p // K, z, yh, p % K)

    def near_chip(p):
        return device(r, zh * ZL + p // YH, p % YH, k)

    def far_block(p):
        return device(r, p * ZL + zl, yh, k)

    def target(q):
        return device(zh, r * ZL + q // YH, q % YH, s // M)

    def source(b):
        s_ = k * M + b
        return device(zh, r * ZL + (s_ // K) // YH, (s_ // K) % YH, s_ % K)

    own = jnp.logical_and(zh == r, s // M == k)
    own_target, own_source = m, s % M

    half = LANES // K
    fetch_a = pltpu.make_async_copy(a_ref, a_in, recv.at[6])
    fetch_b = pltpu.make_async_copy(view_ref, view_in, recv.at[7])
    fetch_a.start()
    fetch_b.start()

    near_steps = {2: (1,), 4: (2, 1, -1), 8: (2, -2, 1, -1)}[ZH]
    far_steps = ((2, (2, 1)), (-2, (-1,))) if ZH == 8 else ()
    seen = {0, *near_steps, *(gone + step for gone, steps in far_steps for step in steps)}
    seen -= {gone for gone, _ in far_steps}

    barrier = pltpu.get_barrier_semaphore()

    def greet(n, me, peer):
        def one(t, c):
            pl.semaphore_signal(barrier, inc=1, device_id=peer(lax.rem(me + t, n)), device_id_type=MESH)
            return c

        lax.fori_loop(1, n, one, 0)

    def greet_across(peer, own_index):
        def one(q, c):
            @pl.when(jnp.logical_not(jnp.logical_and(own, q == own_index)))
            def _():
                pl.semaphore_signal(barrier, inc=1, device_id=peer(q), device_id_type=MESH)

            return c

        lax.fori_loop(0, M, one, 0)

    greet_across(target, own_target)
    greet_across(source, own_source)
    for step in (1, -1, 2, -2)[: min(ZH // 2 * 2 - 1, 4) if ZH < 8 else 4]:
        pl.semaphore_signal(barrier, inc=1, device_id=far_block(lax.rem(zh + step + ZH, ZH)), device_id_type=MESH)
    greet(M, m, near_chip)
    greet(N, rho, near_row)
    fetch_b.wait()
    view_b = view_in[...].astype(f32).T
    b_ref[...] = jnp.concatenate([view_b[:rows], view_b[rows:]], axis=1).astype(bf16)
    fetch_a.wait()
    with jax.named_scope("s0_barrier"):
        pl.semaphore_wait(barrier, 2 * M + min(ZH - 1, 4) + (M - 1) + (N - 1) - 2 * own.astype(jnp.int32))

    def spread(n, me, peer, src, dst, i):
        def one(t, c):
            p = lax.rem(me + t, n)
            pltpu.make_async_remote_copy(
                src_ref=src(p), dst_ref=dst.at[me], send_sem=send.at[i], recv_sem=recv.at[i],
                device_id=peer(p), device_id_type=MESH,
            ).start()
            return c

        lax.fori_loop(1, n, one, 0)
        pltpu.make_async_copy(src(me), dst.at[me], recv.at[i]).start()

    def arrived(dst, i):
        with jax.named_scope(f"w{i}"):
            pltpu.make_async_copy(dst, dst, recv.at[i]).wait()

    def sent(dst, n, i):
        part = dst.at[pl.ds(0, n)]
        pltpu.make_async_copy(part, part, send.at[i]).wait()

    def across(peer, own_index, src, dst, slot, i):
        def one(q, c):
            mine = jnp.logical_and(own, q == own_index)

            @pl.when(mine)
            def _():
                pltpu.make_async_copy(src(q), dst.at[slot], recv.at[i]).start()

            @pl.when(jnp.logical_not(mine))
            def _():
                pltpu.make_async_remote_copy(
                    src_ref=src(q), dst_ref=dst.at[slot], send_sem=send.at[i], recv_sem=recv.at[i],
                    device_id=peer(q), device_id_type=MESH,
                ).start()

            return c

        lax.fori_loop(0, M, one, 0)

    def sent_across(dst, i):
        @pl.when(own)
        def _():
            sent(dst, M - 1, i)

        @pl.when(jnp.logical_not(own))
        def _():
            sent(dst, M, i)

    def block(step):
        return lax.rem(zh + step + ZH, ZH)

    def pass_on(src, dst, i, step, gone):
        pltpu.make_async_remote_copy(
            src_ref=src, dst_ref=dst.at[block(step - (step + gone))], send_sem=ring.at[i],
            recv_sem=hop.at[i, (step + gone) % ZH], device_id=far_block(block(step)), device_id_type=MESH,
        ).start()

    def came(dst, i, gone):
        with jax.named_scope(f"h{i}_{gone % ZH}"):
            slot = dst.at[block(-gone)]
            pltpu.make_async_copy(slot, slot, hop.at[i, gone % ZH]).wait()

    def blocks_start(src, dst, i):
        pltpu.make_async_copy(src, dst.at[zh], hop.at[i, 0]).start()
        for step in near_steps:
            pass_on(src, dst, i, step, 0)

    def blocks_forward(dst, i):
        for gone, steps in far_steps:
            came(dst, i, gone)
            for step in steps:
                pass_on(dst.at[block(-gone)], dst, i, step, gone)

    def blocks_end(dst, i):
        for gone in (0, *(g for g in (1, -1, 2, 3, 4, -3) if g % ZH and abs(g) <= ZH // 2)):
            if gone in seen:
                came(dst, i, gone)

    def columns(q):
        return a_in.at[:, pl.ds(pl.multiple_of(q * LANES, LANES), LANES)]

    across(target, own_target, columns, ta, own_source, 0)
    spread(N, rho, near_row, lambda p: b_ref, pb, 1)

    def normalize(normed):
        values = xf[...]
        center = jnp.sum(values, 0, keepdims=True) / images
        shifted = values - center
        spread_ = jnp.sum(shifted * shifted, 0, keepdims=True) / images
        scaled = lax.rsqrt(spread_ + epsilon)
        normed[...] = (shifted * scaled).astype(bf16)
        return scaled

    own_rows = pl.ds(pl.multiple_of(rho * rows, rows), rows)

    def gram(normed, out):
        g = lax.dot_general(
            normed[own_rows, :], normed[...], (((1,), (1,)), ((), ())), preferred_element_type=f32
        )
        out[:, :, :images] = g.reshape(M, SUB, images).astype(bf16)

    def parts_of(v):
        high = v.astype(bf16).astype(f32)
        middle = (v - high).astype(bf16).astype(f32)
        return tile_of(high, middle, v - high - middle).astype(bf16)

    def summed(parts):
        return functools.reduce(jnp.add, [parts[i].astype(f32) for i in range(parts.shape[0])])

    line = lax.broadcasted_iota(jnp.int32, (SUB, LANES), 0)

    def term_of(rg, normed, other):
        g = rg[...].astype(f32).reshape(rows, images)
        product = jnp.dot(g.astype(bf16), normed[...], preferred_element_type=f32)
        return (2.0 * off_weight / images) * product + other * d, g

    def tile_of(*lines):
        out = jnp.zeros((SUB, LANES), f32)
        for i, v in enumerate(lines):
            out = jnp.where(line == i, jnp.broadcast_to(v, out.shape), out)
        return out

    def projected(term, mine, scaled, first, second):
        return scaled * (term - first / images - mine * (second / images))

    arrived(pb, 1)
    low = lax.broadcasted_iota(jnp.int32, (rows, LANES), 1) < half
    for i in range(R):
        p0, p1 = pb[2 * i].astype(f32), pb[2 * i + 1].astype(f32)
        xf[pl.ds(2 * i * rows, rows), :] = jnp.where(low, p0, pltpu.roll(p1, half, 1))
        xf[pl.ds((2 * i + 1) * rows, rows), :] = jnp.where(low, pltpu.roll(p0, half, 1), p1)
    scaled_b = normalize(nb)
    gram(nb, gp_b)
    spread(M, m, near_chip, lambda p: gp_b.at[p], ra_b, 2)

    arrived(ta, 0)
    spread(N, rho, near_row, lambda p: ta, xa, 3)

    arrived(ra_b, 2)
    hs_b[...] = summed(ra_b).astype(bf16)
    blocks_start(hs_b, rb_b, 0)

    arrived(xa, 3)
    for i in range(N):
        xf[pl.ds(i * rows, rows), :] = xa[i].astype(f32).reshape(rows, LANES)
    scaled_a = normalize(na)
    gram(na, gp_a)
    corr = jnp.sum(na[...].astype(f32) * nb[...].astype(f32), 0, keepdims=True) / images
    d = 2.0 * (corr - 1.0) - (2.0 * off_weight) * corr
    parts = parts_of(jnp.square(1.0 - corr) - off_weight * jnp.square(corr))
    for i in range(M):
        gp_a[i, :, images:] = parts
    spread(M, m, near_chip, lambda p: gp_a.at[p], ra_a, 4)
    mine_a, mine_b = na[own_rows, :].astype(f32), nb[own_rows, :].astype(f32)
    blocks_forward(rb_b, 0)

    arrived(ra_a, 4)
    near = summed(ra_a)
    hs_a[:, :images] = near[:, :images].astype(bf16)
    hs_a[:, images:] = parts_of(jnp.sum(near[:, images:], 0, keepdims=True))
    blocks_start(hs_a, rb_a, 1)

    blocks_end(rb_b, 0)
    ms_b[...] = summed(rb_b).astype(bf16)
    spread(M, m, near_chip, lambda p: ms_b, rg_b, 9)
    blocks_forward(rb_a, 1)

    arrived(rg_b, 9)
    term_a, g_b = term_of(rg_b, na, mine_b)
    ss_a[...] = tile_of(jnp.sum(term_a, 0, keepdims=True), jnp.sum(term_a * mine_a, 0, keepdims=True))
    spread(N, rho, near_row, lambda p: ss_a, sb_a, 10)

    blocks_end(rb_a, 1)
    whole = summed(rb_a)
    ms_a[...] = whole[:, :images].astype(bf16)
    spread(M, m, near_chip, lambda p: ms_a, rg_a, 12)
    diagonal = jnp.sum(whole[:, images:], 0, keepdims=True)

    arrived(sb_a, 10)
    sums = summed(sb_a)
    grad_a = projected(term_a, mine_a, scaled_a, sums[0:1], sums[1:2])
    fs[...] = grad_a.reshape(M, SUB, LANES).astype(bf16)
    across(source, own_source, lambda b: fs.at[b], fa, own_target, 11)

    arrived(rg_a, 12)
    term_b, g_a = term_of(rg_a, nb, mine_a)
    tb[...] = term_b
    partner = pltpu.make_async_remote_copy(
        src_ref=tb, dst_ref=tp, send_sem=send.at[14], recv_sem=recv.at[14],
        device_id=device(r, z, yh, 1 - k), device_id_type=MESH,
    )
    partner.start()
    ss_b[...] = tile_of(jnp.sum(term_b, 0, keepdims=True), jnp.sum(term_b * mine_b, 0, keepdims=True))
    spread(N, rho, near_row, lambda p: ss_b, sb_b, 13)
    both = jnp.sum(g_a * g_b, 0, keepdims=True)
    trace = functools.reduce(jnp.add, [both[:, i * LANES : (i + 1) * LANES] for i in range(images // LANES)])
    ls[...] = jnp.broadcast_to(trace, ls.shape)
    spread(N, rho, near_row, lambda p: ls, lb, 8)

    other_rows = pl.ds(pl.multiple_of((r * K + 1 - k) * rows, rows), rows)
    with jax.named_scope("w14"):
        partner.wait()
    other_b, other_mine = tp[...], nb[other_rows, :].astype(f32)
    arrived(sb_b, 13)
    sums = summed(sb_b)
    pieces = [
        projected(term, mine, scaled_b, sums[0:1], sums[1:2]).T
        for term, mine in ((term_b, mine_b), (other_b, other_mine))
    ]
    own_t, other_t = (jnp.where(k == 0, v[:half], v[half:]) for v in pieces)
    gb_ref[...] = jnp.where(
        k == 0, jnp.concatenate([own_t, other_t], axis=1), jnp.concatenate([other_t, own_t], axis=1)
    ).astype(bf16)

    arrived(lb, 8)
    each = diagonal + summed(lb)[0:1] * (off_weight / (images * images))
    loss_ref[0, 0] = jnp.sum(each) / features

    arrived(fa, 11)
    for q in range(M):
        ga_ref[:, q * LANES : (q + 1) * LANES] = fa[q]

    sent_across(ta, 0)
    sent_across(fa, 11)
    for i, dst in ((1, pb), (3, xa), (8, lb), (10, sb_a), (13, sb_b)):
        sent(dst, N - 1, i)
    for i, dst in ((2, ra_b), (4, ra_a), (9, rg_b), (12, rg_a)):
        sent(dst, M - 1, i)
    for i, dst in ((0, rb_b), (1, rb_a)):
        part = dst.at[pl.ds(0, ZH - 1)]
        pltpu.make_async_copy(part, part, ring.at[i]).wait()


def hand_over(loss_in, ga_in, gb_in, loss_ref, ga_ref, gb_ref):
    loss_ref[0, 0] = loss_in[0, 0]
    ga_ref[...] = ga_in[...]
    gb_ref[...] = gb_in[...]


def solution_on(split, interpret=False):
    YL, X, Z, YH, _ = split.devices.shape
    R = YL * X
    ZH, ZL = R, Z // R
    M, N = ZL * YH, R * K
    rows = M * SUB
    images = N * rows

    def body(view_a, view_b):
        vmem = pltpu.VMEM
        places = [pl.BlockSpec(memory_space=space) for space in (pltpu.SMEM, pltpu.VMEM, pltpu.VMEM)]
        loss, grad_a, grad_b = pl.pallas_call(
            functools.partial(kernel, X, ZL, YH, ZH),
            out_shape=(
                jax.ShapeDtypeStruct((1, 1), f32),
                jax.ShapeDtypeStruct(view_a.shape, bf16),
                jax.ShapeDtypeStruct(view_b.shape[::-1], bf16),
            ),
            in_specs=[pl.BlockSpec(memory_space=pl.ANY)] * 2,
            out_specs=places,
            scratch_shapes=[
                vmem(view_a.shape, bf16),
                vmem(view_b.shape[::-1], bf16),
                vmem((rows, LANES), bf16),
                vmem((M, SUB, LANES), bf16),
                vmem((N, M, SUB, LANES), bf16),
                vmem((N, rows, LANES), bf16),
                vmem((images, LANES), f32),
                vmem((images, LANES), bf16),
                vmem((images, LANES), bf16),
                vmem((M, SUB, images + LANES), bf16),
                vmem((M, SUB, images), bf16),
                vmem((M, SUB, images + LANES), bf16),
                vmem((M, SUB, images), bf16),
                vmem((SUB, images + LANES), bf16),
                vmem((SUB, images), bf16),
                vmem((ZH, SUB, images + LANES), bf16),
                vmem((ZH, SUB, images), bf16),
                vmem((SUB, images), bf16),
                vmem((SUB, images), bf16),
                vmem((M, SUB, images), bf16),
                vmem((M, SUB, images), bf16),
                vmem((SUB, LANES), f32),
                vmem((N, SUB, LANES), f32),
                vmem((SUB, LANES), f32),
                vmem((N, SUB, LANES), f32),
                vmem((SUB, LANES), f32),
                vmem((N, SUB, LANES), f32),
                vmem((M, SUB, LANES), bf16),
                vmem((M, SUB, LANES), bf16),
                vmem((rows, LANES), f32),
                vmem((rows, LANES), f32),
                pltpu.SemaphoreType.DMA((15,)),
                pltpu.SemaphoreType.DMA((15,)),
                pltpu.SemaphoreType.DMA((2,)),
                pltpu.SemaphoreType.DMA((2, ZH)),
            ],
            compiler_params=pltpu.CompilerParams(collective_id=0, has_side_effects=True),
            interpret=interpret,
        )(view_a, view_b.T)
        shapes = [jax.ShapeDtypeStruct(v.shape, v.dtype) for v in (loss, grad_a, grad_b)]
        loss, grad_a, grad_b = pl.pallas_call(
            hand_over, out_shape=shapes, in_specs=places, out_specs=places, interpret=interpret
        )(loss, grad_a, grad_b)
        return loss.reshape(()), grad_a, grad_b.T

    return jax.shard_map(
        body,
        mesh=split,
        in_specs=(P(COL, ROW), P(ROW, COL)),
        out_specs=(P(), P(COL, ROW), P(ROW, COL)),
        check_vma=False,
    )


def solution(mesh):
    return solution_on(Mesh(mesh.devices.reshape(2, 4, 32, 2, 2), AXES))
```

```python
import functools

import jax
import jax.numpy as jnp
from jax import lax
from jax.experimental import pallas as pl
from jax.experimental.pallas import tpu as pltpu
from jax.sharding import Mesh
from jax.sharding import PartitionSpec as P

AXES = ("yl", "x", "z", "yh", "k")
ROW = ("yl", "x")
COL = ("z", "yh", "k")
MESH = pl.DeviceIdType.MESH

off_weight = 0.0051
epsilon = 1e-05
K = 2
LANES = 128
SUB = 8

f32 = jnp.float32
bf16 = jnp.bfloat16


def kernel(
    X, ZL, YH, ZH,
    a_ref, view_ref, loss_ref, ga_ref, gb_ref,
    a_in, view_in, b_ref, ta, xa, pb, xf, na, nb,
    gp_a, gp_b, ra_a, ra_b, hs_a, hs_b, rb_a, rb_b, ms_a, ms_b, rg_a, rg_b,
    ss_a, sb_a, ss_b, sb_b, ls, lb, fs, fa, tb, tp,
    send, recv, ring, hop, pair,
):
    R, M = ZH, ZL * YH
    N = R * K
    rows = M * SUB
    images = N * rows
    features = ZH * M * LANES
    yl, x, z, yh, k = (lax.axis_index(name) for name in AXES)
    r = yl * X + x
    zh, zl = z // ZL, z % ZL
    rho, m = r * K + k, zl * YH + yh
    s = m * K + k

    def device(r_, z_, yh_, k_):
        return (r_ // X, r_ % X, z_, yh_, k_)

    def near_row(p):
        return device(p // K, z, yh, p % K)

    def near_chip(p):
        return device(r, zh * ZL + p // YH, p % YH, k)

    def far_block(p):
        return device(r, p * ZL + zl, yh, k)

    def target(q):
        return device(zh, r * ZL + q // YH, q % YH, s // M)

    def source(b):
        s_ = k * M + b
        return device(zh, r * ZL + (s_ // K) // YH, (s_ // K) % YH, s_ % K)

    own = jnp.logical_and(zh == r, s // M == k)
    own_target, own_source = m, s % M

    half = LANES // K
    fetch_a = pltpu.make_async_copy(a_ref, a_in, recv.at[6])
    fetch_b = pltpu.make_async_copy(view_ref, view_in, recv.at[7])
    fetch_a.start()
    fetch_b.start()

    near_steps = {2: (1,), 4: (2, 1, -1), 8: (2, -2, 1, -1)}[ZH]
    last = {2: (0, 1), 4: (0, 2, 1, -1), 8: (0, 1, -1, 3, -3, 4)}[ZH]

    barrier = pltpu.get_barrier_semaphore()

    def greet(n, me, peer):
        def one(t, c):
            pl.semaphore_signal(barrier, inc=1, device_id=peer(lax.rem(me + t, n)), device_id_type=MESH)
            return c

        lax.fori_loop(1, n, one, 0)

    def greet_across(peer, own_index):
        def one(q, c):
            @pl.when(jnp.logical_not(jnp.logical_and(own, q == own_index)))
            def _():
                pl.semaphore_signal(barrier, inc=1, device_id=peer(q), device_id_type=MESH)

            return c

        lax.fori_loop(0, M, one, 0)

    greet_across(target, own_target)
    greet_across(source, own_source)
    for step in (1, -1, 2, -2)[: min(ZH // 2 * 2 - 1, 4) if ZH < 8 else 4]:
        pl.semaphore_signal(barrier, inc=1, device_id=far_block(lax.rem(zh + step + ZH, ZH)), device_id_type=MESH)
    greet(M, m, near_chip)
    greet(N, rho, near_row)
    fetch_b.wait()
    view_b = view_in[...].astype(f32).T
    b_ref[...] = jnp.concatenate([view_b[:rows], view_b[rows:]], axis=1).astype(bf16)
    fetch_a.wait()
    with jax.named_scope("s0_barrier"):
        pl.semaphore_wait(barrier, 2 * M + min(ZH - 1, 4) + (M - 1) + (N - 1) - 2 * own.astype(jnp.int32))

    def spread(n, me, peer, src, dst, i):
        def one(t, c):
            p = lax.rem(me + t, n)
            pltpu.make_async_remote_copy(
                src_ref=src(p), dst_ref=dst.at[me], send_sem=send.at[i], recv_sem=recv.at[i],
                device_id=peer(p), device_id_type=MESH,
            ).start()
            return c

        lax.fori_loop(1, n, one, 0)
        pltpu.make_async_copy(src(me), dst.at[me], recv.at[i]).start()

    def arrived(dst, i):
        with jax.named_scope(f"w{i}"):
            pltpu.make_async_copy(dst, dst, recv.at[i]).wait()

    def sent(dst, n, i):
        part = dst.at[pl.ds(0, n)]
        pltpu.make_async_copy(part, part, send.at[i]).wait()

    def gather(src, dst, i):
        spread(R, r, lambda p: device(p, z, yh, k), lambda p: src, dst.at[k], i)

    def swap(dst, i, j):
        arrived(dst.at[k], i)
        copy = pltpu.make_async_remote_copy(
            src_ref=dst.at[k], dst_ref=dst.at[k], send_sem=pair.at[j], recv_sem=pair.at[j + 1],
            device_id=device(r, z, yh, 1 - k), device_id_type=MESH,
        )
        copy.start()
        with jax.named_scope(f"x{i}"):
            copy.wait()

    def across(peer, own_index, src, dst, slot, i):
        def one(q, c):
            mine = jnp.logical_and(own, q == own_index)

            @pl.when(mine)
            def _():
                pltpu.make_async_copy(src(q), dst.at[slot], recv.at[i]).start()

            @pl.when(jnp.logical_not(mine))
            def _():
                pltpu.make_async_remote_copy(
                    src_ref=src(q), dst_ref=dst.at[slot], send_sem=send.at[i], recv_sem=recv.at[i],
                    device_id=peer(q), device_id_type=MESH,
                ).start()

            return c

        lax.fori_loop(0, M, one, 0)

    def sent_across(dst, i):
        @pl.when(own)
        def _():
            sent(dst, M - 1, i)

        @pl.when(jnp.logical_not(own))
        def _():
            sent(dst, M, i)

    def block(step):
        return lax.rem(zh + step + ZH, ZH)

    def came(dst, i, gone):
        with jax.named_scope(f"h{i}_{gone % ZH}"):
            slot = dst.at[block(-gone)]
            pltpu.make_async_copy(slot, slot, hop.at[i, gone % ZH]).wait()

    def blocks_start(src, dst, i):
        pltpu.make_async_copy(src, dst.at[zh], hop.at[i, 0]).start()
        for step in near_steps:
            pltpu.make_async_remote_copy(
                src_ref=src, dst_ref=dst.at[zh], send_sem=ring.at[i], recv_sem=hop.at[i, step % ZH],
                device_id=far_block(block(step)), device_id_type=MESH,
            ).start()

    def hand_on(slot, i, step, mark):
        pltpu.make_async_remote_copy(
            src_ref=slot, dst_ref=slot, send_sem=ring.at[i], recv_sem=hop.at[i, mark],
            device_id=far_block(block(step)), device_id_type=MESH,
        ).start()

    def blocks_forward(dst, i):
        if ZH < 8:
            return
        for nth, turn in enumerate((1 - 2 * k, 2 * k - 1)):
            slot = dst.at[block(-2 * turn)]
            with jax.named_scope(f"f{i}"):
                pltpu.make_async_copy(slot, slot, hop.at[i, lax.rem(2 * turn + ZH, ZH)]).wait()
            if nth == 0:
                hand_on(slot, i, 2 * turn, 4)
            hand_on(slot, i, turn, lax.rem(3 * turn + ZH, ZH))

    def blocks_end(dst, i):
        for gone in last:
            came(dst, i, gone)

    def columns(q):
        return a_in.at[:, pl.ds(pl.multiple_of(q * LANES, LANES), LANES)]

    across(target, own_target, columns, ta, own_source, 0)
    gather(b_ref, pb, 1)

    def normalize(normed):
        values = xf[...]
        center = jnp.sum(values, 0, keepdims=True) / images
        shifted = values - center
        spread_ = jnp.sum(shifted * shifted, 0, keepdims=True) / images
        scaled = lax.rsqrt(spread_ + epsilon)
        normed[...] = (shifted * scaled).astype(bf16)
        return scaled

    own_rows = pl.ds(pl.multiple_of(rho * rows, rows), rows)

    def gram(normed, out):
        g = lax.dot_general(
            normed[own_rows, :], normed[...], (((1,), (1,)), ((), ())), preferred_element_type=f32
        )
        out[:, :, :images] = g.reshape(M, SUB, images).astype(bf16)

    def parts_of(v):
        high = v.astype(bf16).astype(f32)
        middle = (v - high).astype(bf16).astype(f32)
        return tile_of(high, middle, v - high - middle).astype(bf16)

    def summed(parts):
        return functools.reduce(jnp.add, [parts[i].astype(f32) for i in range(parts.shape[0])])

    line = lax.broadcasted_iota(jnp.int32, (SUB, LANES), 0)

    def term_of(rg, normed, other):
        g = rg[...].astype(f32).reshape(rows, images)
        product = jnp.dot(g.astype(bf16), normed[...], preferred_element_type=f32)
        return (2.0 * off_weight / images) * product + other * d, g

    def tile_of(*lines):
        out = jnp.zeros((SUB, LANES), f32)
        for i, v in enumerate(lines):
            out = jnp.where(line == i, jnp.broadcast_to(v, out.shape), out)
        return out

    def projected(term, mine, scaled, first, second):
        return scaled * (term - first / images - mine * (second / images))

    swap(pb, 1, 0)
    low = lax.broadcasted_iota(jnp.int32, (rows, LANES), 1) < half
    for i in range(R):
        p0, p1 = pb[0, i].astype(f32), pb[1, i].astype(f32)
        xf[pl.ds(2 * i * rows, rows), :] = jnp.where(low, p0, pltpu.roll(p1, half, 1))
        xf[pl.ds((2 * i + 1) * rows, rows), :] = jnp.where(low, pltpu.roll(p0, half, 1), p1)
    scaled_b = normalize(nb)
    gram(nb, gp_b)
    spread(M, m, near_chip, lambda p: gp_b.at[p], ra_b, 2)

    arrived(ta, 0)
    gather(ta, xa, 3)

    arrived(ra_b, 2)
    hs_b[...] = summed(ra_b).astype(bf16)
    blocks_start(hs_b, rb_b, 0)

    swap(xa, 3, 2)
    for i in range(N):
        xf[pl.ds(i * rows, rows), :] = xa[i % K, i // K].astype(f32).reshape(rows, LANES)
    scaled_a = normalize(na)
    gram(na, gp_a)
    corr = jnp.sum(na[...].astype(f32) * nb[...].astype(f32), 0, keepdims=True) / images
    d = 2.0 * (corr - 1.0) - (2.0 * off_weight) * corr
    parts = parts_of(jnp.square(1.0 - corr) - off_weight * jnp.square(corr))
    for i in range(M):
        gp_a[i, :, images:] = parts
    spread(M, m, near_chip, lambda p: gp_a.at[p], ra_a, 4)
    mine_a, mine_b = na[own_rows, :].astype(f32), nb[own_rows, :].astype(f32)
    blocks_forward(rb_b, 0)

    arrived(ra_a, 4)
    near = summed(ra_a)
    hs_a[:, :images] = near[:, :images].astype(bf16)
    hs_a[:, images:] = parts_of(jnp.sum(near[:, images:], 0, keepdims=True))
    blocks_start(hs_a, rb_a, 1)

    blocks_end(rb_b, 0)
    ms_b[...] = summed(rb_b).astype(bf16)
    spread(M, m, near_chip, lambda p: ms_b, rg_b, 9)
    blocks_forward(rb_a, 1)

    arrived(rg_b, 9)
    term_a, g_b = term_of(rg_b, na, mine_b)
    ss_a[...] = tile_of(jnp.sum(term_a, 0, keepdims=True), jnp.sum(term_a * mine_a, 0, keepdims=True))
    spread(N, rho, near_row, lambda p: ss_a, sb_a, 10)

    blocks_end(rb_a, 1)
    whole = summed(rb_a)
    ms_a[...] = whole[:, :images].astype(bf16)
    spread(M, m, near_chip, lambda p: ms_a, rg_a, 12)
    diagonal = jnp.sum(whole[:, images:], 0, keepdims=True)

    arrived(sb_a, 10)
    sums = summed(sb_a)
    grad_a = projected(term_a, mine_a, scaled_a, sums[0:1], sums[1:2])
    fs[...] = grad_a.reshape(M, SUB, LANES).astype(bf16)
    across(source, own_source, lambda b: fs.at[b], fa, own_target, 11)

    arrived(rg_a, 12)
    term_b, g_a = term_of(rg_a, nb, mine_a)
    tb[...] = term_b
    partner = pltpu.make_async_remote_copy(
        src_ref=tb, dst_ref=tp, send_sem=send.at[14], recv_sem=recv.at[14],
        device_id=device(r, z, yh, 1 - k), device_id_type=MESH,
    )
    partner.start()
    ss_b[...] = tile_of(jnp.sum(term_b, 0, keepdims=True), jnp.sum(term_b * mine_b, 0, keepdims=True))
    spread(N, rho, near_row, lambda p: ss_b, sb_b, 13)
    both = jnp.sum(g_a * g_b, 0, keepdims=True)
    trace = functools.reduce(jnp.add, [both[:, i * LANES : (i + 1) * LANES] for i in range(images // LANES)])
    ls[...] = jnp.broadcast_to(trace, ls.shape)
    spread(N, rho, near_row, lambda p: ls, lb, 8)

    other_rows = pl.ds(pl.multiple_of((r * K + 1 - k) * rows, rows), rows)
    with jax.named_scope("w14"):
        partner.wait()
    other_b, other_mine = tp[...], nb[other_rows, :].astype(f32)
    arrived(sb_b, 13)
    sums = summed(sb_b)
    pieces = [
        projected(term, mine, scaled_b, sums[0:1], sums[1:2]).T
        for term, mine in ((term_b, mine_b), (other_b, other_mine))
    ]
    own_t, other_t = (jnp.where(k == 0, v[:half], v[half:]) for v in pieces)
    gb_ref[...] = jnp.where(
        k == 0, jnp.concatenate([own_t, other_t], axis=1), jnp.concatenate([other_t, own_t], axis=1)
    ).astype(bf16)

    arrived(lb, 8)
    each = diagonal + summed(lb)[0:1] * (off_weight / (images * images))
    loss_ref[0, 0] = jnp.sum(each) / features

    arrived(fa, 11)
    for q in range(M):
        ga_ref[:, q * LANES : (q + 1) * LANES] = fa[q]

    sent_across(ta, 0)
    sent_across(fa, 11)
    for i, dst in ((1, pb), (3, xa)):
        sent(dst.at[0], R - 1, i)
    for i, dst in ((8, lb), (10, sb_a), (13, sb_b)):
        sent(dst, N - 1, i)
    for i, dst in ((2, ra_b), (4, ra_a), (9, rg_b), (12, rg_a)):
        sent(dst, M - 1, i)
    for i, dst in ((0, rb_b), (1, rb_a)):
        part = dst.at[pl.ds(0, ZH - 1)]
        pltpu.make_async_copy(part, part, ring.at[i]).wait()


def hand_over(loss_in, ga_in, gb_in, loss_ref, ga_ref, gb_ref):
    loss_ref[0, 0] = loss_in[0, 0]
    ga_ref[...] = ga_in[...]
    gb_ref[...] = gb_in[...]


def solution_on(split, interpret=False):
    YL, X, Z, YH, _ = split.devices.shape
    R = YL * X
    ZH, ZL = R, Z // R
    M, N = ZL * YH, R * K
    rows = M * SUB
    images = N * rows

    def body(view_a, view_b):
        vmem = pltpu.VMEM
        places = [pl.BlockSpec(memory_space=space) for space in (pltpu.SMEM, pltpu.VMEM, pltpu.VMEM)]
        loss, grad_a, grad_b = pl.pallas_call(
            functools.partial(kernel, X, ZL, YH, ZH),
            out_shape=(
                jax.ShapeDtypeStruct((1, 1), f32),
                vmem(view_a.shape, bf16),
                vmem(view_b.shape[::-1], bf16),
            ),
            in_specs=[pl.BlockSpec(memory_space=pl.ANY)] * 2,
            out_specs=places,
            scratch_shapes=[
                vmem(view_a.shape, bf16),
                vmem(view_b.shape[::-1], bf16),
                vmem((rows, LANES), bf16),
                vmem((M, SUB, LANES), bf16),
                vmem((K, R, M, SUB, LANES), bf16),
                vmem((K, R, rows, LANES), bf16),
                vmem((images, LANES), f32),
                vmem((images, LANES), bf16),
                vmem((images, LANES), bf16),
                vmem((M, SUB, images + LANES), bf16),
                vmem((M, SUB, images), bf16),
                vmem((M, SUB, images + LANES), bf16),
                vmem((M, SUB, images), bf16),
                vmem((SUB, images + LANES), bf16),
                vmem((SUB, images), bf16),
                vmem((ZH, SUB, images + LANES), bf16),
                vmem((ZH, SUB, images), bf16),
                vmem((SUB, images), bf16),
                vmem((SUB, images), bf16),
                vmem((M, SUB, images), bf16),
                vmem((M, SUB, images), bf16),
                vmem((SUB, LANES), f32),
                vmem((N, SUB, LANES), f32),
                vmem((SUB, LANES), f32),
                vmem((N, SUB, LANES), f32),
                vmem((SUB, LANES), f32),
                vmem((N, SUB, LANES), f32),
                vmem((M, SUB, LANES), bf16),
                vmem((M, SUB, LANES), bf16),
                vmem((rows, LANES), f32),
                vmem((rows, LANES), f32),
                pltpu.SemaphoreType.DMA((15,)),
                pltpu.SemaphoreType.DMA((15,)),
                pltpu.SemaphoreType.DMA((2,)),
                pltpu.SemaphoreType.DMA((2, ZH)),
                pltpu.SemaphoreType.DMA((4,)),
            ],
            compiler_params=pltpu.CompilerParams(collective_id=0, has_side_effects=True),
            interpret=interpret,
        )(view_a, view_b.T)
        shapes = [jax.ShapeDtypeStruct(v.shape, v.dtype) for v in (loss, grad_a, grad_b)]
        loss, grad_a, grad_b = pl.pallas_call(
            hand_over, out_shape=shapes, in_specs=places, out_specs=places, interpret=interpret
        )(loss, *(pltpu.with_memory_space_constraint(v, pltpu.VMEM) for v in (grad_a, grad_b)))
        return loss.reshape(()), grad_a, grad_b.T

    return jax.shard_map(
        body,
        mesh=split,
        in_specs=(P(COL, ROW), P(ROW, COL)),
        out_specs=(P(), P(COL, ROW), P(ROW, COL)),
        check_vma=False,
    )


def solution(mesh):
    return solution_on(Mesh(mesh.devices.reshape(2, 4, 32, 2, 2), AXES))
```

```python
import functools

import jax
import jax.numpy as jnp
from jax import lax
from jax.experimental import pallas as pl
from jax.experimental.pallas import tpu as pltpu
from jax.sharding import Mesh
from jax.sharding import PartitionSpec as P

AXES = ("yl", "x", "z", "yh", "k")
ROW = ("yl", "x")
COL = ("z", "yh", "k")
MESH = pl.DeviceIdType.MESH

off_weight = 0.0051
epsilon = 1e-05
K = 2
LANES = 128
SUB = 8

f32 = jnp.float32
bf16 = jnp.bfloat16


def kernel(
    X, ZL, YH, ZH,
    a_ref, view_ref, loss_ref, ga_ref, gb_ref,
    a_in, view_in, b_ref, ta, xa, pb, xf, na, nb,
    gp_a, gp_b, ra_a, ra_b, hs_a, hs_b, rb_a, rb_b, ms_a, ms_b, rg_a, rg_b,
    ss_a, sb_a, ss_b, sb_b, ls, lb, fs, fa, tb, tp,
    send, recv, ring, hop, pair,
):
    R, M = ZH, ZL * YH
    N = R * K
    rows = M * SUB
    images = N * rows
    features = ZH * M * LANES
    yl, x, z, yh, k = (lax.axis_index(name) for name in AXES)
    r = yl * X + x
    zh, zl = z // ZL, z % ZL
    rho, m = r * K + k, zl * YH + yh
    s = m * K + k

    def device(r_, z_, yh_, k_):
        return (r_ // X, r_ % X, z_, yh_, k_)

    def near_row(p):
        return device(p // K, z, yh, p % K)

    def near_chip(p):
        return device(r, zh * ZL + p // YH, p % YH, k)

    def far_block(p):
        return device(r, p * ZL + zl, yh, k)

    def target(q):
        return device(zh, r * ZL + q // YH, q % YH, s // M)

    def source(b):
        s_ = k * M + b
        return device(zh, r * ZL + (s_ // K) // YH, (s_ // K) % YH, s_ % K)

    own = jnp.logical_and(zh == r, s // M == k)
    own_target, own_source = m, s % M

    half = LANES // K
    fetch_a = pltpu.make_async_copy(a_ref, a_in, recv.at[6])
    fetch_b = pltpu.make_async_copy(view_ref, view_in, recv.at[7])
    fetch_a.start()
    fetch_b.start()

    near_steps = {2: (1,), 4: (2, 1, -1), 8: (2, -2, 1, -1)}[ZH]
    last = {2: (0, 1), 4: (0, 2, 1, -1), 8: (0, 1, -1, 3, -3, 4)}[ZH]

    barrier = pltpu.get_barrier_semaphore()

    def greet(n, me, peer):
        def one(t, c):
            pl.semaphore_signal(barrier, inc=1, device_id=peer(lax.rem(me + t, n)), device_id_type=MESH)
            return c

        lax.fori_loop(1, n, one, 0)

    def greet_across(peer, own_index):
        def one(q, c):
            @pl.when(jnp.logical_not(jnp.logical_and(own, q == own_index)))
            def _():
                pl.semaphore_signal(barrier, inc=1, device_id=peer(q), device_id_type=MESH)

            return c

        lax.fori_loop(0, M, one, 0)

    greet_across(target, own_target)
    greet_across(source, own_source)
    for step in (1, -1, 2, -2)[: min(ZH // 2 * 2 - 1, 4) if ZH < 8 else 4]:
        pl.semaphore_signal(barrier, inc=1, device_id=far_block(lax.rem(zh + step + ZH, ZH)), device_id_type=MESH)
    greet(M, m, near_chip)
    greet(N, rho, near_row)
    fetch_b.wait()
    view_b = view_in[...].astype(f32).T
    b_ref[...] = jnp.concatenate([view_b[:rows], view_b[rows:]], axis=1).astype(bf16)
    fetch_a.wait()
    with jax.named_scope("s0_barrier"):
        pl.semaphore_wait(barrier, 2 * M + min(ZH - 1, 4) + (M - 1) + (N - 1) - 2 * own.astype(jnp.int32))

    def spread(n, me, peer, src, dst, i):
        def one(t, c):
            p = lax.rem(me + t, n)
            pltpu.make_async_remote_copy(
                src_ref=src(p), dst_ref=dst.at[me], send_sem=send.at[i], recv_sem=recv.at[i],
                device_id=peer(p), device_id_type=MESH,
            ).start()
            return c

        lax.fori_loop(1, n, one, 0)
        pltpu.make_async_copy(src(me), dst.at[me], recv.at[i]).start()

    def arrived(dst, i):
        with jax.named_scope(f"w{i}"):
            pltpu.make_async_copy(dst, dst, recv.at[i]).wait()

    def sent(dst, n, i):
        part = dst.at[pl.ds(0, n)]
        pltpu.make_async_copy(part, part, send.at[i]).wait()

    def gather(src, dst, i):
        spread(R, r, lambda p: device(p, z, yh, k), lambda p: src, dst.at[k], i)

    def swap(dst, i, j):
        arrived(dst.at[k], i)
        copy = pltpu.make_async_remote_copy(
            src_ref=dst.at[k], dst_ref=dst.at[k], send_sem=pair.at[j], recv_sem=pair.at[j + 1],
            device_id=device(r, z, yh, 1 - k), device_id_type=MESH,
        )
        copy.start()
        with jax.named_scope(f"x{i}"):
            copy.wait()

    def across(peer, own_index, src, dst, slot, i):
        def one(q, c):
            mine = jnp.logical_and(own, q == own_index)

            @pl.when(mine)
            def _():
                pltpu.make_async_copy(src(q), dst.at[slot], recv.at[i]).start()

            @pl.when(jnp.logical_not(mine))
            def _():
                pltpu.make_async_remote_copy(
                    src_ref=src(q), dst_ref=dst.at[slot], send_sem=send.at[i], recv_sem=recv.at[i],
                    device_id=peer(q), device_id_type=MESH,
                ).start()

            return c

        lax.fori_loop(0, M, one, 0)

    def sent_across(dst, i):
        @pl.when(own)
        def _():
            sent(dst, M - 1, i)

        @pl.when(jnp.logical_not(own))
        def _():
            sent(dst, M, i)

    def block(step):
        return lax.rem(zh + step + ZH, ZH)

    def came(dst, i, gone):
        with jax.named_scope(f"h{i}_{gone % ZH}"):
            slot = dst.at[block(-gone)]
            pltpu.make_async_copy(slot, slot, hop.at[i, gone % ZH]).wait()

    def blocks_start(src, dst, i):
        pltpu.make_async_copy(src, dst.at[zh], hop.at[i, 0]).start()
        for step in near_steps:
            pltpu.make_async_remote_copy(
                src_ref=src, dst_ref=dst.at[zh], send_sem=ring.at[i], recv_sem=hop.at[i, step % ZH],
                device_id=far_block(block(step)), device_id_type=MESH,
            ).start()

    def hand_on(slot, i, step, mark):
        pltpu.make_async_remote_copy(
            src_ref=slot, dst_ref=slot, send_sem=ring.at[i], recv_sem=hop.at[i, mark],
            device_id=far_block(block(step)), device_id_type=MESH,
        ).start()

    def blocks_forward(dst, i):
        if ZH < 8:
            return
        for nth, turn in enumerate((1 - 2 * k, 2 * k - 1)):
            slot = dst.at[block(-2 * turn)]
            with jax.named_scope(f"f{i}"):
                pltpu.make_async_copy(slot, slot, hop.at[i, lax.rem(2 * turn + ZH, ZH)]).wait()
            if nth == 0:
                hand_on(slot, i, 2 * turn, 4)
            hand_on(slot, i, turn, lax.rem(3 * turn + ZH, ZH))

    def blocks_end(dst, i):
        for gone in last:
            came(dst, i, gone)

    def columns(q):
        return a_in.at[:, pl.ds(pl.multiple_of(q * LANES, LANES), LANES)]

    across(target, own_target, columns, ta, own_source, 0)
    gather(b_ref, pb, 1)

    def normalize(normed):
        values = xf[...]
        center = jnp.sum(values, 0, keepdims=True) / images
        shifted = values - center
        spread_ = jnp.sum(shifted * shifted, 0, keepdims=True) / images
        scaled = lax.rsqrt(spread_ + epsilon)
        normed[...] = (shifted * scaled).astype(bf16)
        return scaled

    own_rows = pl.ds(pl.multiple_of(rho * rows, rows), rows)

    def gram(normed, out):
        g = lax.dot_general(
            normed[own_rows, :], normed[...], (((1,), (1,)), ((), ())), preferred_element_type=f32
        )
        out[:, :, :images] = g.reshape(M, SUB, images).astype(bf16)

    def parts_of(v):
        high = v.astype(bf16).astype(f32)
        middle = (v - high).astype(bf16).astype(f32)
        return tile_of(high, middle, v - high - middle).astype(bf16)

    def summed(parts):
        return functools.reduce(jnp.add, [parts[i].astype(f32) for i in range(parts.shape[0])])

    line = lax.broadcasted_iota(jnp.int32, (SUB, LANES), 0)

    def term_of(rg, normed, other):
        g = rg[...].astype(f32).reshape(rows, images)
        product = jnp.dot(g.astype(bf16), normed[...], preferred_element_type=f32)
        return (2.0 * off_weight / images) * product + other * d, g

    def tile_of(*lines):
        out = jnp.zeros((SUB, LANES), f32)
        for i, v in enumerate(lines):
            out = jnp.where(line == i, jnp.broadcast_to(v, out.shape), out)
        return out

    def sums_of(term, mine):
        return jnp.concatenate([jnp.sum(v, 0, keepdims=True) for v in (term, term * mine)], axis=0)

    def projected(term, mine, scaled, first, second):
        return scaled * (term - first / images - mine * (second / images))

    swap(pb, 1, 0)
    low = lax.broadcasted_iota(jnp.int32, (rows, LANES), 1) < half
    for i in range(R):
        p0, p1 = pb[0, i].astype(f32), pb[1, i].astype(f32)
        xf[pl.ds(2 * i * rows, rows), :] = jnp.where(low, p0, pltpu.roll(p1, half, 1))
        xf[pl.ds((2 * i + 1) * rows, rows), :] = jnp.where(low, pltpu.roll(p0, half, 1), p1)
    scaled_b = normalize(nb)
    gram(nb, gp_b)
    spread(M, m, near_chip, lambda p: gp_b.at[p], ra_b, 2)

    arrived(ta, 0)
    gather(ta, xa, 3)

    arrived(ra_b, 2)
    hs_b[...] = summed(ra_b).astype(bf16)
    blocks_start(hs_b, rb_b, 0)

    swap(xa, 3, 2)
    for i in range(N):
        xf[pl.ds(i * rows, rows), :] = xa[i % K, i // K].astype(f32).reshape(rows, LANES)
    scaled_a = normalize(na)
    gram(na, gp_a)
    corr = jnp.sum(na[...].astype(f32) * nb[...].astype(f32), 0, keepdims=True) / images
    d = 2.0 * (corr - 1.0) - (2.0 * off_weight) * corr
    parts = parts_of(jnp.square(1.0 - corr) - off_weight * jnp.square(corr))
    for i in range(M):
        gp_a[i, :, images:] = parts
    spread(M, m, near_chip, lambda p: gp_a.at[p], ra_a, 4)
    mine_a, mine_b = na[own_rows, :].astype(f32), nb[own_rows, :].astype(f32)
    blocks_forward(rb_b, 0)

    arrived(ra_a, 4)
    near = summed(ra_a)
    hs_a[:, :images] = near[:, :images].astype(bf16)
    hs_a[:, images:] = parts_of(jnp.sum(near[:, images:], 0, keepdims=True))
    blocks_start(hs_a, rb_a, 1)

    blocks_end(rb_b, 0)
    ms_b[...] = summed(rb_b).astype(bf16)
    spread(M, m, near_chip, lambda p: ms_b, rg_b, 9)
    blocks_forward(rb_a, 1)

    arrived(rg_b, 9)
    term_a, g_b = term_of(rg_b, na, mine_b)
    ss_a[...] = sums_of(term_a, mine_a)
    spread(N, rho, near_row, lambda p: ss_a, sb_a, 10)

    blocks_end(rb_a, 1)
    whole = summed(rb_a)
    ms_a[...] = whole[:, :images].astype(bf16)
    spread(M, m, near_chip, lambda p: ms_a, rg_a, 12)
    diagonal = jnp.sum(whole[:, images:], 0, keepdims=True)

    arrived(sb_a, 10)
    sums = summed(sb_a)
    grad_a = projected(term_a, mine_a, scaled_a, sums[0:1], sums[1:2])
    fs[...] = grad_a.reshape(M, SUB, LANES).astype(bf16)
    across(source, own_source, lambda b: fs.at[b], fa, own_target, 11)

    arrived(rg_a, 12)
    term_b, g_a = term_of(rg_a, nb, mine_a)
    tb[...] = term_b
    partner = pltpu.make_async_remote_copy(
        src_ref=tb, dst_ref=tp, send_sem=send.at[14], recv_sem=recv.at[14],
        device_id=device(r, z, yh, 1 - k), device_id_type=MESH,
    )
    partner.start()
    ss_b[...] = sums_of(term_b, mine_b)
    spread(N, rho, near_row, lambda p: ss_b, sb_b, 13)
    both = jnp.sum(g_a * g_b, 0, keepdims=True)
    trace = functools.reduce(jnp.add, [both[:, i * LANES : (i + 1) * LANES] for i in range(images // LANES)])
    ls[...] = trace
    spread(N, rho, near_row, lambda p: ls, lb, 8)

    other_rows = pl.ds(pl.multiple_of((r * K + 1 - k) * rows, rows), rows)
    with jax.named_scope("w14"):
        partner.wait()
    other_b, other_mine = tp[...], nb[other_rows, :].astype(f32)
    arrived(sb_b, 13)
    sums = summed(sb_b)
    pieces = [
        projected(term, mine, scaled_b, sums[0:1], sums[1:2]).T
        for term, mine in ((term_b, mine_b), (other_b, other_mine))
    ]
    own_t, other_t = (jnp.where(k == 0, v[:half], v[half:]) for v in pieces)
    gb_ref[...] = jnp.where(
        k == 0, jnp.concatenate([own_t, other_t], axis=1), jnp.concatenate([other_t, own_t], axis=1)
    ).astype(bf16)

    arrived(lb, 8)
    each = diagonal + summed(lb)[0:1] * (off_weight / (images * images))
    loss_ref[0, 0] = jnp.sum(each) / features

    sent_across(ta, 0)
    sent_across(fa, 11)
    for i, dst in ((1, pb), (3, xa)):
        sent(dst.at[0], R - 1, i)
    for i, dst in ((8, lb), (10, sb_a), (13, sb_b)):
        sent(dst, N - 1, i)
    for i, dst in ((2, ra_b), (4, ra_a), (9, rg_b), (12, rg_a)):
        sent(dst, M - 1, i)
    for i, dst in ((0, rb_b), (1, rb_a)):
        part = dst.at[pl.ds(0, ZH - 1)]
        pltpu.make_async_copy(part, part, ring.at[i]).wait()

    arrived(fa, 11)
    for q in range(M):
        ga_ref[:, q * LANES : (q + 1) * LANES] = fa[q]


def hand_over(loss_in, ga_in, gb_in, loss_ref, ga_ref, gb_ref):
    loss_ref[0, 0] = loss_in[0, 0]
    ga_ref[...] = ga_in[...]
    gb_ref[...] = gb_in[...]


def solution_on(split, interpret=False):
    YL, X, Z, YH, _ = split.devices.shape
    R = YL * X
    ZH, ZL = R, Z // R
    M, N = ZL * YH, R * K
    rows = M * SUB
    images = N * rows

    def body(view_a, view_b):
        vmem = pltpu.VMEM
        places = [pl.BlockSpec(memory_space=space) for space in (pltpu.SMEM, pltpu.VMEM, pltpu.VMEM)]
        loss, grad_a, grad_b = pl.pallas_call(
            functools.partial(kernel, X, ZL, YH, ZH),
            out_shape=(
                jax.ShapeDtypeStruct((1, 1), f32),
                vmem(view_a.shape, bf16),
                vmem(view_b.shape[::-1], bf16),
            ),
            in_specs=[pl.BlockSpec(memory_space=pl.ANY)] * 2,
            out_specs=places,
            scratch_shapes=[
                vmem(view_a.shape, bf16),
                vmem(view_b.shape[::-1], bf16),
                vmem((rows, LANES), bf16),
                vmem((M, SUB, LANES), bf16),
                vmem((K, R, M, SUB, LANES), bf16),
                vmem((K, R, rows, LANES), bf16),
                vmem((images, LANES), f32),
                vmem((images, LANES), bf16),
                vmem((images, LANES), bf16),
                vmem((M, SUB, images + LANES), bf16),
                vmem((M, SUB, images), bf16),
                vmem((M, SUB, images + LANES), bf16),
                vmem((M, SUB, images), bf16),
                vmem((SUB, images + LANES), bf16),
                vmem((SUB, images), bf16),
                vmem((ZH, SUB, images + LANES), bf16),
                vmem((ZH, SUB, images), bf16),
                vmem((SUB, images), bf16),
                vmem((SUB, images), bf16),
                vmem((M, SUB, images), bf16),
                vmem((M, SUB, images), bf16),
                vmem((2, LANES), f32),
                vmem((N, 2, LANES), f32),
                vmem((2, LANES), f32),
                vmem((N, 2, LANES), f32),
                vmem((1, LANES), f32),
                vmem((N, 1, LANES), f32),
                vmem((M, SUB, LANES), bf16),
                vmem((M, SUB, LANES), bf16),
                vmem((rows, LANES), f32),
                vmem((rows, LANES), f32),
                pltpu.SemaphoreType.DMA((15,)),
                pltpu.SemaphoreType.DMA((15,)),
                pltpu.SemaphoreType.DMA((2,)),
                pltpu.SemaphoreType.DMA((2, ZH)),
                pltpu.SemaphoreType.DMA((4,)),
            ],
            compiler_params=pltpu.CompilerParams(collective_id=0, has_side_effects=True),
            interpret=interpret,
        )(view_a, view_b.T)
        shapes = [jax.ShapeDtypeStruct(v.shape, v.dtype) for v in (loss, grad_a, grad_b)]
        loss, grad_a, grad_b = pl.pallas_call(
            hand_over, out_shape=shapes, in_specs=places, out_specs=places, interpret=interpret
        )(loss, *(pltpu.with_memory_space_constraint(v, pltpu.VMEM) for v in (grad_a, grad_b)))
        return loss.reshape(()), grad_a, grad_b.T

    return jax.shard_map(
        body,
        mesh=split,
        in_specs=(P(COL, ROW), P(ROW, COL)),
        out_specs=(P(), P(COL, ROW), P(ROW, COL)),
        check_vma=False,
    )


def solution(mesh):
    return solution_on(Mesh(mesh.devices.reshape(2, 4, 32, 2, 2), AXES))
```
